32 devices in a mesh: dp: 8 (over z, x), head: 4 (over y, core).
Axes of the slice: x: 2, y: 2, z: 4, core: 2. Of those that a mesh axis runs over, the one named last changes fastest.
Arguments:
- latents: bfloat16 [32, 128, 1024], P('dp', 'head'), may hold values from -6 to 6
- inputs: bfloat16 [32, 512, 1024], P('dp', 'head'), may hold values from -6 to 6
- input_masks: int32 [32, 512], P('dp'), may hold values 0 or 1
- valid_counts: int32 [32], P('dp'), may hold values from 1 to 512
- gain_input: float32 [1024], replicated, may hold values from 0.5 to 1.5
- gain_cross: float32 [1024], replicated, may hold values from 0.5 to 1.5
- gain_self: float32 [1024], replicated, may hold values from 0.5 to 1.5
- gain_mlp: float32 [1024], replicated, may hold values from 0.5 to 1.5
- query_cross: bfloat16 [1024, 1024], P('dp', 'head'), may hold values from -0.375 to 0.375
- key_cross: bfloat16 [1024, 1024], P('dp', 'head'), may hold values from -0.1875 to 0.1875
- value_cross: bfloat16 [1024, 1024], P('dp', 'head'), may hold values from -0.1875 to 0.1875
- output_cross: bfloat16 [1024, 1024], P('head', 'dp'), may hold values from -0.75 to 0.75
- query_self: bfloat16 [1024, 1024], P('dp', 'head'), may hold values from -0.375 to 0.375
- key_self: bfloat16 [1024, 1024], P('dp', 'head'), may hold values from -0.1875 to 0.1875
- value_self: bfloat16 [1024, 1024], P('dp', 'head'), may hold values from -0.1875 to 0.1875
- output_self: bfloat16 [1024, 1024], P('head', 'dp'), may hold values from -0.75 to 0.75
- mlp_up: bfloat16 [1024, 4096], P('dp', 'head'), may hold values from -0.1875 to 0.1875
- mlp_down: bfloat16 [4096, 1024], P('head', 'dp'), may hold values from -0.09375 to 0.09375
- out_cotangent: bfloat16 [32, 128, 1024], P('dp', 'head'), may hold values from -6 to 6
Outputs:
- block_out: bfloat16 [32, 128, 1024], P('dp', 'head')
- grad_latents: float32 [32, 128, 1024], P('dp', 'head')
- grad_inputs: float32 [32, 512, 1024], P('dp', 'head')
- grad_gain_input: float32 [1024], replicated
- grad_gain_cross: float32 [1024], replicated
- grad_gain_self: float32 [1024], replicated
- grad_gain_mlp: float32 [1024], replicated
- grad_query_cross: float32 [1024, 1024], P('dp', 'head')
- grad_key_cross: float32 [1024, 1024], P('dp', 'head')
- grad_value_cross: float32 [1024, 1024], P('dp', 'head')
- grad_output_cross: float32 [1024, 1024], P('head', 'dp')
- grad_query_self: float32 [1024, 1024], P('dp', 'head')
- grad_key_self: float32 [1024, 1024], P('dp', 'head')
- grad_value_self: float32 [1024, 1024], P('dp', 'head')
- grad_output_self: float32 [1024, 1024], P('head', 'dp')
- grad_mlp_up: float32 [1024, 4096], P('dp', 'head')
- grad_mlp_down: float32 [4096, 1024], P('head', 'dp')
The draws below stay inside these ranges and needn't reach their ends.
All inputs are finite; a program needn't handle non-finite values. No bound on the sum of `input_masks` on one device may be relied on, other than what follows from the above.
Results may differ from the reference program's by a relative error of at most 0.038.
Values may be sent and summed in bfloat16 or wider, within the bound.
A program may use at most 128 MiB of HBM per device.

```python
from functools import partial
import jax
import jax.numpy as jnp
from jax import lax

D = 1024
HEAD_DIM = 128
FF = 4096
LATENTS = 128
INPUT_ROWS = 512
GROUPS = 32


def draw_valid_counts(key, part):
    keys_split = jax.random.split(key, 4)
    broad = jax.random.randint(keys_split[0], (GROUPS,), INPUT_ROWS // 4, INPUT_ROWS + 1)
    sparse = jax.random.randint(keys_split[1], (GROUPS,), 1, 17)
    picker = jax.random.randint(keys_split[2], (GROUPS,), 0, 4)
    counts_drawn = jnp.where(picker == 0, sparse, broad)
    fullest = jax.random.randint(keys_split[3], (), 0, GROUPS)
    return jnp.where(jnp.arange(GROUPS, dtype=jnp.int32) == fullest, INPUT_ROWS, counts_drawn).astype(jnp.int32)


def set_ends(array, key, smallest, high):
    spot = [jax.random.randint(jax.random.fold_in(key, axis), (), 0, length) for axis, length in enumerate(array.shape)]
    longest = array.shape.index(max(array.shape))
    neighbour = spot[:longest] + [(spot[longest] + 1) % array.shape[longest]] + spot[longest + 1:]
    return array.at[tuple(spot)].set(smallest).at[tuple(neighbour)].set(high)


def level_of(rng, extent, pieces, low, largest):
    factor_of, own = 1.0, jax.random.fold_in(rng, 6)
    for position, parts in pieces:
        steps = jnp.exp(jax.random.uniform(jax.random.fold_in(own, position), (parts,), jnp.float32, low / len(pieces), largest / len(pieces)))
        factor_of = factor_of * jnp.repeat(steps, extent[position] // parts).reshape([-1 if axis == position else 1 for axis in range(len(extent))])
    return factor_of


def scatter_about(stream_key, extent, scale, limit, shards=(), held_as=jnp.bfloat16):
    drawn = scale * jax.random.normal(stream_key, extent, jnp.float32)
    if shards:
        drawn = drawn * level_of(stream_key, extent, shards, -0.22, 0.18)
    return jnp.clip(drawn, -limit, limit).astype(held_as)


def setup_inputs(seed: int = 0) -> dict:
    seeds = jax.random.split(jax.random.key(seed), 20)
    latents = scatter_about(seeds[0], (GROUPS, LATENTS, D), 1.0, 6.0, ((0, 8), (1, 4)))
    inputs = scatter_about(seeds[1], (GROUPS, INPUT_ROWS, D), 1.0, 6.0, ((0, 8), (1, 4)))
    input_masks = set_ends((jax.random.randint(seeds[2], (GROUPS, INPUT_ROWS), 0, 4) < 3).astype(jnp.int32), jax.random.fold_in(seeds[2], 1), 0, 1)
    valid_counts = draw_valid_counts(jax.random.fold_in(seeds[19], 71), 0)
    gain_input = jnp.clip(1.0 + 0.1 * jax.random.normal(seeds[4], (D,), jnp.float32), 0.5, 1.5)
    gain_cross = jnp.clip(1.0 + 0.1 * jax.random.normal(seeds[5], (D,), jnp.float32), 0.5, 1.5)
    gain_self = jnp.clip(1.0 + 0.1 * jax.random.normal(seeds[6], (D,), jnp.float32), 0.5, 1.5)
    gain_mlp = jnp.clip(1.0 + 0.1 * jax.random.normal(seeds[7], (D,), jnp.float32), 0.5, 1.5)
    query_cross = scatter_about(seeds[8], (D, D), (D // 4) ** -0.5, 0.375, ((0, 8), (1, 4)))
    key_cross = scatter_about(seeds[9], (D, D), D ** -0.5, 0.1875, ((0, 8), (1, 4)))
    value_cross = scatter_about(seeds[10], (D, D), D ** -0.5, 0.1875, ((0, 8), (1, 4)))
    output_cross = scatter_about(seeds[11], (D, D), (D // 16) ** -0.5, 0.75, ((0, 4), (1, 8)))
    query_self = scatter_about(seeds[12], (D, D), (D // 4) ** -0.5, 0.375, ((0, 8), (1, 4)))
    key_self = scatter_about(seeds[13], (D, D), D ** -0.5, 0.1875, ((0, 8), (1, 4)))
    value_self = scatter_about(seeds[14], (D, D), D ** -0.5, 0.1875, ((0, 8), (1, 4)))
    output_self = scatter_about(seeds[15], (D, D), (D // 16) ** -0.5, 0.75, ((0, 4), (1, 8)))
    mlp_up = scatter_about(seeds[16], (D, FF), D ** -0.5, 0.1875, ((0, 8), (1, 4)))
    mlp_down = scatter_about(seeds[17], (FF, D), FF ** -0.5, 0.09375, ((0, 4), (1, 8)))
    out_cotangent = scatter_about(seeds[18], (GROUPS, LATENTS, D), 1.0, 6.0, ((0, 8), (1, 4)))
    return dict(latents=latents, inputs=inputs, input_masks=input_masks, valid_counts=valid_counts, gain_input=gain_input, gain_cross=gain_cross, gain_self=gain_self, gain_mlp=gain_mlp, query_cross=query_cross, key_cross=key_cross, value_cross=value_cross, output_cross=output_cross, query_self=query_self, key_self=key_self, value_self=value_self, output_self=output_self, mlp_up=mlp_up, mlp_down=mlp_down, out_cotangent=out_cotangent)


@jax.custom_vjp
def low(v):
    return lax.optimization_barrier(v.astype(jnp.bfloat16)).astype(jnp.float32)

@jax.custom_vjp
def low_back(v):
    return v

def low_keep(v):
    return (low(v), None)

def low_pass(kept, grad):
    return (grad,)

def back_keep(v):
    return (v, None)

def back_low(kept, grad):
    return (low(grad),)
low.defvjp(low_keep, low_pass)
low_back.defvjp(back_keep, back_low)
epsilon = 1e-05
highest = lax.Precision.HIGHEST

def layer_norm(row_data, gain_vec):
    row_mean = lax.optimization_barrier(jnp.mean(row_data, axis=-1, keepdims=True))
    centered = row_data - row_mean
    row_var = lax.optimization_barrier(jnp.mean(centered * centered, axis=-1, keepdims=True))
    return centered * lax.rsqrt(row_var + epsilon) * gain_vec

def project(row_data, weight):
    return jnp.einsum('gnd,de->gne', row_data, weight, precision=highest)

def split_heads(tensor):
    return tensor.reshape(tensor.shape[0], tensor.shape[1], -1, HEAD_DIM)

def attend(queries, key_rows, values, allowed):
    scores = jnp.einsum('gqhe,gkhe->ghqk', split_heads(queries), split_heads(key_rows), precision=highest) * HEAD_DIM ** (-0.5)
    if allowed is not None:
        scores = jnp.where(allowed[:, None, None, :], scores, -1e+30)
    scores = low_back(scores)
    prob_low = low(jax.nn.softmax(scores, axis=-1))
    attended = jnp.einsum('ghqk,gkhe->gqhe', prob_low, split_heads(values), precision=highest)
    return attended.reshape(queries.shape)

def group_block(weights, gains, latent_rows, input_rows, allowed):
    query_cross, key_cross, value_cross, output_cross, query_self, key_self, value_self, output_self, mlp_up, mlp_down = weights
    gain_input, gain_cross, gain_self, gain_mlp = gains
    normed_lat = low(layer_norm(latent_rows, gain_cross))
    normed_in = low(layer_norm(input_rows, gain_input))
    queries = low_back(low(project(normed_lat, query_cross)))
    key_rows = low_back(low(project(normed_in, key_cross)))
    values = low_back(low(project(normed_in, value_cross)))
    attended = low_back(low(attend(queries, key_rows, values, allowed)))
    hidden_one = latent_rows + low_back(project(attended, output_cross))
    normed_two = low(layer_norm(hidden_one, gain_self))
    queries_two = low_back(low(project(normed_two, query_self)))
    keys_two = low_back(low(project(normed_two, key_self)))
    values_two = low_back(low(project(normed_two, value_self)))
    attended_two = low_back(low(attend(queries_two, keys_two, values_two, None)))
    hidden_two = hidden_one + low_back(project(attended_two, output_self))
    normed_three = low(layer_norm(hidden_two, gain_mlp))
    pre_act = low_back(project(normed_three, mlp_up))
    activated = low(jax.nn.gelu(pre_act, approximate=True))
    return hidden_two + low_back(project(activated, mlp_down))

def forward(weights, gains, latents_f, inputs_f, allowed):
    batch_groups = 8
    blocks = latents_f.shape[0] // batch_groups
    step_fn = jax.checkpoint(partial(group_block, weights, gains))

    def run_block(packed):
        return step_fn(packed[0], packed[1], packed[2])
    outputs = lax.map(run_block, (latents_f.reshape(blocks, batch_groups, LATENTS, D), inputs_f.reshape(blocks, batch_groups, INPUT_ROWS, D), allowed.reshape(blocks, batch_groups, INPUT_ROWS)))
    return outputs.reshape(latents_f.shape)

def reference(latents, inputs, input_masks, valid_counts, gain_input, gain_cross, gain_self, gain_mlp, query_cross, key_cross, value_cross, output_cross, query_self, key_self, value_self, output_self, mlp_up, mlp_down, out_cotangent):
    positions = jnp.arange(INPUT_ROWS, dtype=jnp.int32)
    allowed = (positions[None, :] < valid_counts[:, None]) & ((input_masks == 1) | (positions[None, :] == 0))
    weights = (query_cross.astype(jnp.float32), key_cross.astype(jnp.float32), value_cross.astype(jnp.float32), output_cross.astype(jnp.float32), query_self.astype(jnp.float32), key_self.astype(jnp.float32), value_self.astype(jnp.float32), output_self.astype(jnp.float32), mlp_up.astype(jnp.float32), mlp_down.astype(jnp.float32))
    gains = (gain_input, gain_cross, gain_self, gain_mlp)

    def whole(weight_set, gain_set, latents_f, inputs_f):
        return forward(weight_set, gain_set, latents_f, inputs_f, allowed)
    result, pullback = jax.vjp(whole, weights, gains, latents.astype(jnp.float32), inputs.astype(jnp.float32))
    grad_weights, grad_gains, grad_latents, grad_inputs = pullback(out_cotangent.astype(jnp.float32))
    return (result.astype(jnp.bfloat16), grad_latents, grad_inputs, grad_gains[0], grad_gains[1], grad_gains[2], grad_gains[3], grad_weights[0], grad_weights[1], grad_weights[2], grad_weights[3], grad_weights[4], grad_weights[5], grad_weights[6], grad_weights[7], grad_weights[8], grad_weights[9])
```

```python
import functools

import jax
import jax.numpy as jnp
from jax import lax
from jax.experimental import pallas as pl
from jax.experimental.pallas import tpu as pltpu
from jax.sharding import PartitionSpec as P

HEAD_DIM = 128
CHUNK = 256
PAIR = 2
MESH = pl.DeviceIdType.MESH

epsilon = 1e-05


def layer_norm(row_data, gain_vec):
    row_mean = jnp.mean(row_data, axis=-1, keepdims=True)
    centered = row_data - row_mean
    row_var = jnp.mean(centered * centered, axis=-1, keepdims=True)
    return centered * lax.rsqrt(row_var + epsilon) * gain_vec


def norm_back(row_data, gain_vec, cotangent):
    result, pullback = jax.vjp(layer_norm, row_data, gain_vec)
    return pullback(cotangent)


def gelu_back(pre_act, cotangent):
    result, pullback = jax.vjp(lambda values: jax.nn.gelu(values, approximate=True), pre_act)
    return pullback(cotangent)[0]


def project(row_data, weight):
    return jnp.einsum("gnd,de->gne", row_data, weight, preferred_element_type=jnp.float32)


def project_t(row_data, weight):
    return jnp.einsum("gne,de->gnd", row_data, weight, preferred_element_type=jnp.float32)


def weight_grad(row_data, gradients):
    return jnp.einsum(
        "gnd,gne->de", row_data, gradients, preferred_element_type=jnp.float32
    ).astype(jnp.bfloat16)


def split_heads(tensor):
    return tensor.reshape(tensor.shape[0], tensor.shape[1], -1, HEAD_DIM)


def score_rows(queries, key_rows, allowed):
    scores = jnp.einsum(
        "gqhe,gkhe->ghqk",
        split_heads(queries),
        split_heads(key_rows),
        preferred_element_type=jnp.float32,
    ) * HEAD_DIM ** (-0.5)
    if allowed is not None:
        scores = jnp.where(allowed[:, None, None, :], scores, -1e30)
    return scores


def attend_forward(queries, key_rows, values, allowed):
    scores = score_rows(queries, key_rows, allowed)
    log_total = jax.scipy.special.logsumexp(scores, axis=-1, keepdims=True)
    prob_low = jnp.exp(scores - log_total).astype(jnp.bfloat16)
    attended = jnp.einsum(
        "ghqk,gkhe->gqhe", prob_low, split_heads(values), preferred_element_type=jnp.float32
    )
    return (attended.astype(jnp.bfloat16).reshape(queries.shape), log_total)


def attend_backward(queries, key_rows, values, allowed, log_total, grad_attended):
    scaling = HEAD_DIM ** (-0.5)
    prob_full = jnp.exp(score_rows(queries, key_rows, allowed) - log_total)
    grad_heads = split_heads(grad_attended)
    grad_probs = jnp.einsum(
        "gqhe,gkhe->ghqk", grad_heads, split_heads(values), preferred_element_type=jnp.float32
    )
    row_delta = jnp.sum(grad_probs * prob_full, axis=-1, keepdims=True)
    grad_scores = (prob_full * (grad_probs - row_delta)).astype(jnp.bfloat16)
    grad_query = jnp.einsum(
        "ghqk,gkhe->gqhe", grad_scores, split_heads(key_rows), preferred_element_type=jnp.float32
    )
    grad_keys = jnp.einsum(
        "ghqk,gqhe->gkhe", grad_scores, split_heads(queries), preferred_element_type=jnp.float32
    )
    grad_values = jnp.einsum(
        "ghqk,gqhe->gkhe",
        prob_full.astype(jnp.bfloat16),
        grad_heads,
        preferred_element_type=jnp.float32,
    )
    grad_query = (grad_query * scaling).astype(jnp.bfloat16).reshape(queries.shape)
    grad_keys = (grad_keys * scaling).astype(jnp.bfloat16).reshape(key_rows.shape)
    grad_values = grad_values.astype(jnp.bfloat16).reshape(values.shape)
    return (grad_query, grad_keys, grad_values)


def grid_place(members):
    me = lax.axis_index("dp")
    line = members // PAIR
    return me, line, me // PAIR, me % PAIR


def greet(members):
    me, line, row, column = grid_place(members)
    barrier = pltpu.get_barrier_semaphore()

    def hello(step, carry):
        peer = lax.rem(row + step, line) * PAIR + column
        pl.semaphore_signal(barrier, inc=1, device_id={"dp": peer}, device_id_type=MESH)
        return carry

    lax.fori_loop(1, line, hello, 0)
    partner = row * PAIR + 1 - column
    pl.semaphore_signal(barrier, inc=1, device_id={"dp": partner}, device_id_type=MESH)
    pl.semaphore_wait(barrier, line)


def push(source, target, send_sem, recv_sem, member):
    pltpu.make_async_remote_copy(
        src_ref=source,
        dst_ref=target,
        send_sem=send_sem,
        recv_sem=recv_sem,
        device_id={"dp": member},
        device_id_type=MESH,
    ).start()


def drain(like, sem):
    pltpu.make_async_copy(like, like, sem).wait()


def gather_kernel(members, shard, full, own_sem, line_send, line_recv, pair_send, pair_recv):
    chunks, rows, width = shard.shape
    me, line, row, column = grid_place(members)
    partner = row * PAIR + 1 - column
    greet(members)
    keep = pltpu.make_async_copy(shard, full.at[:, pl.ds(me * rows, rows), :], own_sem)
    keep.start()

    def block(chunk, member):
        return full.at[chunk, pl.ds(pl.multiple_of(member * rows, rows), rows), :]

    def send_line(chunk, carry):
        def one(step, inner):
            peer = lax.rem(row + step, line) * PAIR + column
            push(shard.at[chunk], block(chunk, me), line_send.at[chunk], line_recv.at[chunk], peer)
            return inner

        return lax.fori_loop(1, line, one, carry)

    def send_pair(chunk, carry):
        push(shard.at[chunk], block(chunk, me), pair_send.at[chunk], pair_recv.at[chunk], partner)
        return carry

    def forward(chunk, carry):
        drain(full.at[chunk, pl.ds(0, (line - 1) * rows), :], line_recv.at[chunk])

        def one(step, inner):
            source = block(chunk, lax.rem(row + step, line) * PAIR + column)
            push(source, source, pair_send.at[chunk], pair_recv.at[chunk], partner)
            return inner

        return lax.fori_loop(1, line, one, carry)

    lax.fori_loop(0, chunks, send_line, 0)
    ahead = min(2, chunks)
    for chunk in range(ahead):
        send_pair(chunk, 0)

    def step(chunk, carry):
        forward(chunk, carry)

        @pl.when(chunk + ahead < chunks)
        def _():
            send_pair(chunk + ahead, 0)

        return carry

    lax.fori_loop(0, chunks, step, 0)

    def finish(chunk, carry):
        drain(full.at[chunk, pl.ds(0, line * rows), :], pair_recv.at[chunk])
        drain(full.at[chunk, pl.ds(0, line * rows), :], pair_send.at[chunk])
        drain(full.at[chunk, pl.ds(0, (line - 1) * rows), :], line_send.at[chunk])
        return carry

    lax.fori_loop(0, chunks, finish, 0)
    keep.wait()


def scatter_kernel(
    members, partial, total, pair_buf, line_buf, line_out, line_send, line_recv, pair_send, pair_recv
):
    chunks, rows, width = total.shape
    me, line, row, column = grid_place(members)
    partner = row * PAIR + 1 - column
    greet(members)

    def part(chunk, member):
        return pl.ds(pl.multiple_of(member * rows, rows), rows)

    def send_pair(chunk, carry):
        def one(other, inner):
            source = partial.at[chunk, part(chunk, other * PAIR + 1 - column), :]
            target = pair_buf.at[chunk, part(chunk, other), :]
            push(source, target, pair_send.at[chunk], pair_recv.at[chunk], partner)
            return inner

        return lax.fori_loop(0, line, one, carry)

    lax.fori_loop(0, chunks, send_pair, 0)

    def send_line(chunk, carry):
        drain(pair_buf.at[chunk], pair_recv.at[chunk])
        own = partial[chunk, part(chunk, me), :].astype(jnp.float32)
        total[chunk] = own + pair_buf[chunk, part(chunk, row), :].astype(jnp.float32)

        def one(step, inner):
            other = lax.rem(row + step, line)
            mine = partial[chunk, part(chunk, other * PAIR + column), :].astype(jnp.float32)
            theirs = pair_buf[chunk, part(chunk, other), :].astype(jnp.float32)
            line_out[chunk, part(chunk, step - 1), :] = (mine + theirs).astype(jnp.bfloat16)
            push(
                line_out.at[chunk, part(chunk, step - 1), :],
                line_buf.at[chunk, part(chunk, step - 1), :],
                line_send.at[chunk],
                line_recv.at[chunk],
                other * PAIR + column,
            )
            return inner

        return lax.fori_loop(1, line, one, carry)

    lax.fori_loop(0, chunks, send_line, 0)

    def finish(chunk, carry):
        drain(line_buf.at[chunk], line_recv.at[chunk])

        def one(step, inner):
            total[chunk] += line_buf[chunk, part(chunk, step - 1), :].astype(jnp.float32)
            return inner

        lax.fori_loop(1, line, one, 0)
        drain(pair_buf.at[chunk], pair_send.at[chunk])
        drain(line_buf.at[chunk], line_send.at[chunk])
        return carry

    lax.fori_loop(0, chunks, finish, 0)


VMEM_SPEC = pl.BlockSpec(memory_space=pltpu.VMEM)
VMEM_TOP = 64 * 1024 * 1024 - 128 * 1024


def gather_weights(members, shard):
    chunks, rows, width = shard.shape
    return pl.pallas_call(
        functools.partial(gather_kernel, members),
        out_shape=jax.ShapeDtypeStruct((chunks, rows * members, width), shard.dtype),
        in_specs=[VMEM_SPEC],
        out_specs=VMEM_SPEC,
        scratch_shapes=[pltpu.SemaphoreType.DMA] + [pltpu.SemaphoreType.DMA((chunks,))] * 4,
        compiler_params=pltpu.CompilerParams(
            collective_id=0, has_side_effects=True, vmem_limit_bytes=32 * 1024 * 1024
        ),
    )(shard)


def scatter_grads(members, partial):
    chunks, depth, width = partial.shape
    rows = depth // members
    line = members // PAIR
    return pl.pallas_call(
        functools.partial(scatter_kernel, members),
        out_shape=jax.ShapeDtypeStruct((chunks, rows, width), jnp.float32),
        in_specs=[VMEM_SPEC],
        out_specs=VMEM_SPEC,
        scratch_shapes=[
            pltpu.VMEM((chunks, line * rows, width), jnp.bfloat16),
            pltpu.VMEM((chunks, (line - 1) * rows, width), jnp.bfloat16),
            pltpu.VMEM((chunks, (line - 1) * rows, width), jnp.bfloat16),
        ]
        + [pltpu.SemaphoreType.DMA((chunks,))] * 4,
        compiler_params=pltpu.CompilerParams(
            collective_id=1, has_side_effects=True, vmem_limit_bytes=48 * 1024 * 1024
        ),
    )(partial)


def to_chunks(matrix):
    rows, width = matrix.shape
    return matrix.reshape(rows, width // CHUNK, CHUNK).transpose(1, 0, 2)


def from_chunks(chunked):
    return chunked.transpose(1, 0, 2).reshape(chunked.shape[1], -1)


def per_device(
    members,
    latents,
    inputs,
    input_masks,
    valid_counts,
    gain_input,
    gain_cross,
    gain_self,
    gain_mlp,
    query_cross,
    key_cross,
    value_cross,
    output_cross,
    query_self,
    key_self,
    value_self,
    output_self,
    mlp_up,
    mlp_down,
    out_cotangent,
):
    by_rows = (
        query_cross,
        key_cross,
        value_cross,
        output_cross.T,
        query_self,
        key_self,
        value_self,
        output_self.T,
        mlp_up,
        mlp_down.T,
    )
    widths = [weight.shape[1] for weight in by_rows]
    gathered = gather_weights(members, to_chunks(jnp.concatenate(by_rows, axis=1)))
    weights = []
    first = 0
    for width in widths:
        weights.append(from_chunks(gathered[first : first + width // CHUNK]))
        first += width // CHUNK

    def spread(row_data):
        return lax.all_gather(row_data, "head", axis=1, tiled=True)

    def fold(partial_rows):
        return lax.psum_scatter(
            partial_rows.astype(jnp.bfloat16), "head", scatter_dimension=1, tiled=True
        ).astype(jnp.float32)

    positions = jnp.arange(input_masks.shape[1], dtype=jnp.int32)
    lat_rows = latents.astype(jnp.float32)
    in_rows = inputs.astype(jnp.float32)
    allowed = (positions[None, :] < valid_counts[:, None]) & (
        (input_masks == 1) | (positions[None, :] == 0)
    )
    full_lat = spread(layer_norm(lat_rows, gain_cross).astype(jnp.bfloat16))
    full_in = spread(layer_norm(in_rows, gain_input).astype(jnp.bfloat16))
    branch_out = spread(out_cotangent)
    queries = project(full_lat, weights[0]).astype(jnp.bfloat16)
    key_rows = project(full_in, weights[1]).astype(jnp.bfloat16)
    values = project(full_in, weights[2]).astype(jnp.bfloat16)
    attended, total_cross = attend_forward(queries, key_rows, values, allowed)
    hidden_one = lat_rows + fold(project_t(attended, weights[3]))
    normed_two = spread(layer_norm(hidden_one, gain_self).astype(jnp.bfloat16))
    queries_two = project(normed_two, weights[4]).astype(jnp.bfloat16)
    keys_two = project(normed_two, weights[5]).astype(jnp.bfloat16)
    values_two = project(normed_two, weights[6]).astype(jnp.bfloat16)
    attended_two, total_self = attend_forward(queries_two, keys_two, values_two, None)
    hidden_two = hidden_one + fold(project_t(attended_two, weights[7]))
    normed_three = spread(layer_norm(hidden_two, gain_mlp).astype(jnp.bfloat16))
    pre_act = project(normed_three, weights[8])
    activated = jax.nn.gelu(pre_act, approximate=True).astype(jnp.bfloat16)
    block_out = (hidden_two + fold(project_t(activated, weights[9]))).astype(jnp.bfloat16)

    grad_out = out_cotangent.astype(jnp.float32)
    grad_down = weight_grad(branch_out, activated)
    grad_pre = gelu_back(pre_act, project(branch_out, weights[9])).astype(jnp.bfloat16)
    grad_up = weight_grad(normed_three, grad_pre)
    back_two, gain_grad_mlp = norm_back(
        hidden_two, gain_mlp, fold(project_t(grad_pre, weights[8]))
    )
    grad_hidden_two = grad_out + back_two
    branch_two = spread(grad_hidden_two.astype(jnp.bfloat16))
    grad_out_self = weight_grad(branch_two, attended_two)
    grad_att_two = project(branch_two, weights[7]).astype(jnp.bfloat16)
    grad_q_two, grad_k_two, grad_v_two = attend_backward(
        queries_two, keys_two, values_two, None, total_self, grad_att_two
    )
    grad_qs = weight_grad(normed_two, grad_q_two)
    grad_ks = weight_grad(normed_two, grad_k_two)
    grad_vs = weight_grad(normed_two, grad_v_two)
    grad_norm_two = fold(
        project_t(grad_q_two, weights[4])
        + project_t(grad_k_two, weights[5])
        + project_t(grad_v_two, weights[6])
    )
    back_one, gain_grad_self = norm_back(hidden_one, gain_self, grad_norm_two)
    grad_hidden_one = grad_hidden_two + back_one
    branch_one = spread(grad_hidden_one.astype(jnp.bfloat16))
    grad_out_cross = weight_grad(branch_one, attended)
    grad_att_one = project(branch_one, weights[3]).astype(jnp.bfloat16)
    grad_q_one, grad_k_one, grad_v_one = attend_backward(
        queries, key_rows, values, allowed, total_cross, grad_att_one
    )
    grad_qc = weight_grad(full_lat, grad_q_one)
    grad_kc = weight_grad(full_in, grad_k_one)
    grad_vc = weight_grad(full_in, grad_v_one)
    grad_lat_norm = fold(project_t(grad_q_one, weights[0]))
    grad_in_norm = fold(project_t(grad_k_one, weights[1]) + project_t(grad_v_one, weights[2]))
    back_lat, gain_grad_cross = norm_back(lat_rows, gain_cross, grad_lat_norm)
    back_in, gain_grad_input = norm_back(in_rows, gain_input, grad_in_norm)
    gain_sums = lax.psum(
        (gain_grad_input, gain_grad_cross, gain_grad_self, gain_grad_mlp), ("dp", "head")
    )
    parts = [
        to_chunks(part)
        for part in (
            grad_qc,
            grad_kc,
            grad_vc,
            grad_out_cross,
            grad_qs,
            grad_ks,
            grad_vs,
            grad_out_self,
            grad_up,
            grad_down,
        )
    ]
    summed = scatter_grads(members, jnp.concatenate(parts, axis=0))
    grads = []
    first = 0
    for width in widths:
        grads.append(from_chunks(summed[first : first + width // CHUNK]))
        first += width // CHUNK
    for turned in (3, 7, 9):
        grads[turned] = grads[turned].T
    return (block_out, grad_hidden_one + back_lat, back_in, *gain_sums, *grads)


def solution(mesh):
    rows_first = P("dp", "head")
    cols_first = P("head", "dp")
    tokens = P("dp", "head", None)
    weight_specs = (
        rows_first,
        rows_first,
        rows_first,
        cols_first,
        rows_first,
        rows_first,
        rows_first,
        cols_first,
        rows_first,
        cols_first,
    )
    in_specs = (tokens, tokens, P("dp", None), P("dp"), P(), P(), P(), P(), *weight_specs, tokens)
    out_specs = (tokens, tokens, tokens, P(), P(), P(), P(), *weight_specs)
    return jax.shard_map(
        functools.partial(per_device, mesh.shape["dp"]),
        mesh=mesh,
        in_specs=in_specs,
        out_specs=out_specs,
        check_vma=False,
    )
```

```python
import functools

import jax
import jax.numpy as jnp
from jax import lax
from jax.experimental import pallas as pl
from jax.experimental.pallas import tpu as pltpu
from jax.sharding import PartitionSpec as P

HEAD_DIM = 128
CHUNK = 256
PAIR = 2
CORES = 2
MESH = pl.DeviceIdType.MESH
VMEM_TOP = 64 * 1024 * 1024 - 64 * 1024

QC, KC, VC, OC, QS, KS, VS, OS, UP = 0, 1, 2, 3, 4, 5, 6, 7, 8

bf16 = jnp.bfloat16
f32 = jnp.float32
epsilon = 1e-05


def dot(left, right):
    return lax.dot_general(left, right, (((1,), (0,)), ((), ())), preferred_element_type=f32)


def dot_t(left, right):
    return lax.dot_general(left, right, (((1,), (1,)), ((), ())), preferred_element_type=f32)


def t_dot(left, right):
    return lax.dot_general(left, right, (((0,), (0,)), ((), ())), preferred_element_type=f32)


def norm_parts(rows):
    centered = rows - jnp.mean(rows, axis=-1, keepdims=True)
    scale = lax.rsqrt(jnp.mean(centered * centered, axis=-1, keepdims=True) + epsilon)
    return centered * scale, scale


def gelu_parts(pre):
    bend = 0.7978845608028654 * (pre + 0.044715 * pre * pre * pre)
    return 0.5 * (1.0 + jnp.tanh(bend))


def gelu_slope(pre):
    squared = pre * pre
    tanh = jnp.tanh(0.7978845608028654 * (pre + 0.044715 * pre * squared))
    inner = 0.7978845608028654 * (1.0 + 3 * 0.044715 * squared)
    return 0.5 * (1.0 + tanh) + 0.5 * pre * (1.0 - tanh * tanh) * inner


def loop(count, body):
    def step(index, carry):
        body(index)
        return carry

    lax.fori_loop(0, count, step, 0)


def flat(value):
    return value.reshape(-1, value.shape[-1])


def push(source, target, send_sem, recv_sem, place):
    pltpu.make_async_remote_copy(
        src_ref=source,
        dst_ref=target,
        send_sem=send_sem,
        recv_sem=recv_sem,
        device_id=place,
        device_id_type=MESH,
    ).start()


def drain(like, sem):
    pltpu.make_async_copy(like, like, sem).wait()


NAMES = (
    "lat",
    "inp",
    "cot",
    "allow",
    "gains",
    "shard",
    "block_out",
    "grad_lat",
    "grad_in",
    "grad_gain",
    "grad_w",
    "full_w",
    "part_w",
    "pair_buf",
    "line_buf",
    "normed_in",
    "normed_lat",
    "normed_two",
    "normed_three",
    "keys",
    "grad_keys",
    "q_one",
    "o_one",
    "q_two",
    "k_two",
    "v_two",
    "o_two",
    "gq_one",
    "gq_two",
    "gk_two",
    "gv_two",
    "grad_att",
    "prob_one",
    "prob_two",
    "pre",
    "act",
    "grad_pre",
    "spread_out",
    "spread_two",
    "spread_one",
    "hidden_one",
    "hidden_two",
    "grad_two",
    "grad_one",
    "partial",
    "partial_out",
    "fold_core",
    "fold_row",
    "in_core",
    "in_row",
    "gain_mine",
    "gain_sum",
    "gain_recv",
    "gain_line",
    "own_sem",
    "gather_sems",
    "scatter_sems",
    "spread_sems",
    "fold_sems",
    "in_sems",
    "in_fold_sems",
    "gain_sems",
)


def block_kernel(members, *refs):
    r = dict(zip(NAMES, refs, strict=True))
    groups, own_lat, depth = r["lat"].shape
    own_in = r["inp"].shape[1]
    hidden = r["act"].shape[2]
    chunks, rows, width = r["shard"].shape
    heads = width // HEAD_DIM
    downs = hidden // width
    down = UP + downs
    scaling = HEAD_DIM ** (-0.5)

    me = lax.axis_index("dp")
    line = members // PAIR
    row, column = me // PAIR, me % PAIR
    partner = {"dp": row * PAIR + 1 - column}
    spot = lax.axis_index("head")
    side, core = spot // CORES, spot % CORES
    spot_core = side * CORES + 1 - core
    spot_row = (1 - side) * CORES + core
    spot_both = (1 - side) * CORES + 1 - core
    to_core = {"head": spot_core}
    to_row = {"head": spot_row}

    def line_peer(step):
        return lax.rem(row + step, line)

    def member(other):
        return {"dp": other * PAIR + column}

    barrier = pltpu.get_barrier_semaphore()
    for place in (partner, to_core, to_row):
        pl.semaphore_signal(barrier, inc=1, device_id=place, device_id_type=MESH)

    def hello(step, carry):
        pl.semaphore_signal(
            barrier, inc=1, device_id=member(line_peer(step)), device_id_type=MESH
        )
        return carry

    lax.fori_loop(1, line, hello, 0)
    pl.semaphore_wait(barrier, line + 2)

    full_w, part_w = r["full_w"], r["part_w"]
    gather_sems, scatter_sems = r["gather_sems"], r["scatter_sems"]

    def block(chunk, other):
        return full_w.at[chunk, pl.ds(pl.multiple_of(other * rows, rows), rows), :]

    def gather_line(chunk):
        def one(step, carry):
            push(
                r["shard"].at[chunk],
                block(chunk, me),
                gather_sems.at[0, chunk],
                gather_sems.at[1, chunk],
                member(line_peer(step)),
            )
            return carry

        lax.fori_loop(1, line, one, 0)

    def gather_pair(chunk):
        push(
            r["shard"].at[chunk],
            block(chunk, me),
            gather_sems.at[2, chunk],
            gather_sems.at[3, chunk],
            partner,
        )

    def gather_forward(chunk):
        drain(full_w.at[chunk, pl.ds(0, (line - 1) * rows), :], gather_sems.at[1, chunk])

        def one(step, carry):
            source = block(chunk, line_peer(step) * PAIR + column)
            push(source, source, gather_sems.at[2, chunk], gather_sems.at[3, chunk], partner)
            return carry

        lax.fori_loop(1, line, one, 0)
        if chunk + ahead < chunks:
            gather_pair(chunk + ahead)

    def have_weights(chunk):
        drain(full_w.at[chunk, pl.ds(0, line * rows), :], gather_sems.at[3, chunk])

    ahead = min(3, chunks)

    def part(index):
        return pl.ds(pl.multiple_of(index * rows, rows), rows)

    pair_buf, line_buf, total = r["pair_buf"], r["line_buf"], r["grad_w"]

    def scatter_pair(chunk):
        def one(other):
            push(
                part_w.at[chunk, part(other * PAIR + 1 - column), :],
                pair_buf.at[chunk, part(other), :],
                scatter_sems.at[0, chunk],
                scatter_sems.at[1, chunk],
                partner,
            )

        loop(line, one)

    def scatter_line(chunk):
        drain(pair_buf.at[chunk], scatter_sems.at[1, chunk])
        own = part_w[chunk, part(me), :].astype(f32)
        total[chunk] = own + pair_buf[chunk, part(row), :].astype(f32)

        def one(step, carry):
            other = line_peer(step)
            mine = part_w[chunk, part(other * PAIR + column), :].astype(f32)
            theirs = pair_buf[chunk, part(other), :].astype(f32)
            pair_buf[chunk, part(other), :] = (mine + theirs).astype(bf16)
            push(
                pair_buf.at[chunk, part(other), :],
                line_buf.at[chunk, part(step - 1), :],
                scatter_sems.at[2, chunk],
                scatter_sems.at[3, chunk],
                member(other),
            )
            return carry

        lax.fori_loop(1, line, one, 0)

    def scatter_end(chunk):
        drain(line_buf.at[chunk], scatter_sems.at[3, chunk])

        def one(step, carry):
            total[chunk] += line_buf[chunk, part(step - 1), :].astype(f32)
            return carry

        lax.fori_loop(1, line, one, 0)

    spread_sems, fold_sems = r["spread_sems"], r["fold_sems"]

    def mine(spot_at):
        return pl.ds(pl.multiple_of(spot_at * own_lat, own_lat), own_lat)

    def mine_in(spot_at):
        return pl.ds(pl.multiple_of(spot_at * own_in, own_in), own_in)

    def spread_first(full, use):
        own = full.at[:, mine(spot), :]
        push(own, own, spread_sems.at[use, 0], spread_sems.at[use, 1], to_row)
        push(own, own, spread_sems.at[use, 2], spread_sems.at[use, 3], to_core)

    def spread_next(full, use):
        got = full.at[:, mine(spot_row), :]
        drain(got, spread_sems.at[use, 1])
        push(got, got, spread_sems.at[use, 4], spread_sems.at[use, 5], to_core)

    def spread_last(full, use):
        drain(full.at[:, mine(spot), :], spread_sems.at[use, 3])
        drain(full.at[:, mine(spot), :], spread_sems.at[use, 5])

    def spread_sent(full, use):
        for which in (0, 2, 4):
            drain(full.at[:, mine(spot), :], spread_sems.at[use, which])

    fold_core, fold_row = r["fold_core"], r["fold_row"]

    def fold_first(whole, use):
        for slot, spot_at in enumerate((spot_core, spot_both)):
            push(
                whole.at[:, mine(spot_at), :],
                fold_core.at[use % 3, slot],
                fold_sems.at[use, 0],
                fold_sems.at[use, 1],
                to_core,
            )

    def fold_next(whole, use):
        drain(fold_core.at[use % 3], fold_sems.at[use, 1])

        def one(group):
            near = whole[group, mine(spot_row), :].astype(f32)
            far = fold_core[use % 3, 1, group].astype(f32)
            whole[group, mine(spot_row), :] = (near + far).astype(bf16)

        loop(groups, one)
        push(
            whole.at[:, mine(spot_row), :],
            fold_row.at[use % 3],
            fold_sems.at[use, 2],
            fold_sems.at[use, 3],
            to_row,
        )

    def fold_last(use):
        drain(fold_row.at[use % 3], fold_sems.at[use, 3])

    def folded(whole, use, group):
        near = whole[group, mine(spot), :].astype(f32) + fold_core[use % 3, 0, group].astype(f32)
        return near + fold_row[use % 3, group].astype(f32)

    def fold_sent(use):
        drain(fold_core.at[use % 3], fold_sems.at[use, 0])
        drain(fold_row.at[use % 3], fold_sems.at[use, 2])

    in_sems, in_fold_sems = r["in_sems"], r["in_fold_sems"]
    normed_in = r["normed_in"]

    def in_first(group):
        own = normed_in.at[group, mine_in(spot), :]
        push(own, own, in_sems.at[group, 0], in_sems.at[group, 1], to_row)
        push(own, own, in_sems.at[group, 2], in_sems.at[group, 3], to_core)

    def in_next(group):
        got = normed_in.at[group, mine_in(spot_row), :]
        drain(got, in_sems.at[group, 1])
        push(got, got, in_sems.at[group, 4], in_sems.at[group, 5], to_core)

    def in_last(group):
        like = normed_in.at[group, mine_in(spot), :]
        drain(like, in_sems.at[group, 3])
        drain(like, in_sems.at[group, 5])

    def in_sent(group):
        for which in (0, 2, 4):
            drain(normed_in.at[group, mine_in(spot), :], in_sems.at[group, which])

    in_core, in_row = r["in_core"], r["in_row"]

    def in_fold_first(group):
        for slot, spot_at in enumerate((spot_core, spot_both)):
            push(
                normed_in.at[group, mine_in(spot_at), :],
                in_core.at[group, slot],
                in_fold_sems.at[group, 0],
                in_fold_sems.at[group, 1],
                to_core,
            )

    def in_fold_next(group):
        drain(in_core.at[group], in_fold_sems.at[group, 1])
        near = normed_in[group, mine_in(spot_row), :].astype(f32)
        normed_in[group, mine_in(spot_row), :] = (
            near + in_core[group, 1].astype(f32)
        ).astype(bf16)
        push(
            normed_in.at[group, mine_in(spot_row), :],
            in_row.at[group],
            in_fold_sems.at[group, 2],
            in_fold_sems.at[group, 3],
            to_row,
        )

    lat, inp, cot = r["lat"], r["inp"], r["cot"]
    gains = r["gains"]
    pairs = 2 if groups % 2 == 0 else 1
    tiles = groups // pairs

    def gain(index):
        return gains[index : index + 1, :]

    def tile(index):
        return pl.ds(index * pairs, pairs)

    def lanes(index, size=width):
        return pl.ds(pl.multiple_of(index * size, size), size)

    def project(target, source, chunk):
        def one(index):
            value = dot(flat(source[tile(index)]), full_w[chunk])
            target[tile(index)] = value.astype(bf16).reshape(pairs, -1, width)

        loop(tiles, one)

    def project_back(target, terms):
        def one(index):
            at, piece = index // (depth // width), index % (depth // width)
            value = None
            for source, first, chunk in terms:
                term = dot_t(
                    flat(source[tile(at), :, first : first + width]),
                    full_w[chunk, lanes(piece), :],
                )
                value = term if value is None else value + term
            target[tile(at), :, lanes(piece)] = value.astype(bf16).reshape(pairs, -1, width)

        loop(tiles * (depth // width), one)

    def weight_grad(chunk, left, right, first=0):
        def one(index):
            value = None
            for group in range(0, groups, pairs):
                for_rows = pl.ds(group, pairs)
                term = t_dot(
                    flat(left[for_rows, :, lanes(index)]),
                    flat(right[for_rows, :, first : first + width]),
                )
                value = term if value is None else value + term
            part_w[chunk, lanes(index), :] = value.astype(bf16)

        loop(depth // width, one)
        scatter_pair(chunk)

    def attend(group, queries, keys, key_at, values, value_at, prob, target, masked):
        for head in range(heads):
            at = head * HEAD_DIM
            query = queries[group, :, at : at + HEAD_DIM]
            key = keys[group, :, key_at + at : key_at + at + HEAD_DIM]
            value = values[group, :, value_at + at : value_at + at + HEAD_DIM]
            scores = dot_t(query, key) * scaling
            if masked:
                scores = jnp.where(r["allow"][group] > 0.5, scores, -1e30)
            grown = jnp.exp(scores - jnp.max(scores, axis=-1, keepdims=True))
            share = grown / jnp.sum(grown, axis=-1, keepdims=True)
            prob[group, head] = share
            target[group, :, at : at + HEAD_DIM] = dot(share.astype(bf16), value).astype(bf16)

    def attend_back(group, queries, keys, key_at, values, value_at, prob, grad, outs):
        (gq, gk, gk_at, gv, gv_at) = outs
        for head in range(heads):
            at = head * HEAD_DIM
            query = queries[group, :, at : at + HEAD_DIM]
            key = keys[group, :, key_at + at : key_at + at + HEAD_DIM]
            value = values[group, :, value_at + at : value_at + at + HEAD_DIM]
            back = grad[group, :, at : at + HEAD_DIM]
            share = prob[group, head]
            slope = dot_t(back, value)
            slope = share * (slope - jnp.sum(share * slope, axis=-1, keepdims=True))
            slope = slope.astype(bf16)
            gq[group, :, at : at + HEAD_DIM] = (dot(slope, key) * scaling).astype(bf16)
            gk[group, :, gk_at + at : gk_at + at + HEAD_DIM] = (
                t_dot(slope, query) * scaling
            ).astype(bf16)
            gv[group, :, gv_at + at : gv_at + at + HEAD_DIM] = t_dot(
                share.astype(bf16), back
            ).astype(bf16)

    gain_mine = r["gain_mine"]
    gain_mine[...] = jnp.zeros_like(gain_mine)

    def norm_back(rows_in, index, grad):
        shaped, scale = norm_parts(rows_in)
        gain_mine[index : index + 1, :] += jnp.sum(grad * shaped, axis=0, keepdims=True)
        grad = grad * gain(index)
        center = jnp.mean(grad, axis=-1, keepdims=True)
        along = jnp.mean(grad * shaped, axis=-1, keepdims=True)
        return (grad - center - shaped * along) * scale

    GAIN_INPUT, GAIN_CROSS, GAIN_SELF, GAIN_MLP = 0, 1, 2, 3

    keep = pltpu.make_async_copy(
        r["shard"], full_w.at[:, pl.ds(pl.multiple_of(me * rows, rows), rows), :], r["own_sem"]
    )
    keep.start()
    loop(chunks, gather_line)
    for chunk in range(ahead):
        gather_pair(chunk)

    def lat_rows(group):
        shaped, _ = norm_parts(lat[group].astype(f32))
        r["normed_lat"][group, mine(spot), :] = (shaped * gain(GAIN_CROSS)).astype(bf16)

    loop(groups, lat_rows)
    spread_first(r["normed_lat"], 0)

    def in_rows(group):
        shaped, _ = norm_parts(inp[group].astype(f32))
        normed_in[group, mine_in(spot), :] = (shaped * gain(GAIN_INPUT)).astype(bf16)
        in_first(group)

    loop(groups, in_rows)
    r["spread_out"][:, mine(spot), :] = cot[...]
    spread_first(r["spread_out"], 3)
    spread_next(r["normed_lat"], 0)
    gather_forward(0)
    for group in range(groups):
        in_next(group)
        if group % 2 == 1:
            gather_forward(1 + group // 2)
    spread_next(r["spread_out"], 3)
    gather_forward(3)
    keep.wait()
    spread_last(r["normed_lat"], 0)
    have_weights(QC)
    project(r["q_one"], r["normed_lat"], QC)
    have_weights(KC)
    gather_forward(4)
    have_weights(VC)
    keys = r["keys"]

    def key_rows(group):
        in_last(group)
        for piece in range(keys.shape[1] // 256):
            at = slice(piece * 256, piece * 256 + 256)
            keys[group, at, :width] = dot(normed_in[group, at, :], full_w[KC]).astype(bf16)
            keys[group, at, width:] = dot(normed_in[group, at, :], full_w[VC]).astype(bf16)
        attend(
            group, r["q_one"], keys, 0, keys, width, r["prob_one"], r["o_one"], True
        )

    loop(groups, key_rows)
    gather_forward(5)
    have_weights(OC)
    project_back(r["partial"], [(r["o_one"], 0, OC)])
    fold_first(r["partial"], 0)
    gather_forward(6)
    fold_next(r["partial"], 0)
    gather_forward(7)
    fold_last(0)

    def one_rows(group):
        rows_now = lat[group].astype(f32) + folded(r["partial"], 0, group)
        r["hidden_one"][group] = rows_now
        shaped, _ = norm_parts(rows_now)
        r["normed_two"][group, mine(spot), :] = (shaped * gain(GAIN_SELF)).astype(bf16)

    loop(groups, one_rows)
    spread_first(r["normed_two"], 1)
    gather_forward(8)
    spread_next(r["normed_two"], 1)
    gather_forward(9)
    spread_last(r["normed_two"], 1)
    for target, chunk in (("q_two", QS), ("k_two", KS), ("v_two", VS)):
        have_weights(chunk)
        project(r[target], r["normed_two"], chunk)

    def self_rows(group):
        attend(
            group,
            r["q_two"],
            r["k_two"],
            0,
            r["v_two"],
            0,
            r["prob_two"],
            r["o_two"],
            False,
        )

    loop(groups, self_rows)
    gather_forward(10)
    have_weights(OS)
    fold_sent(0)
    project_back(r["partial"], [(r["o_two"], 0, OS)])
    fold_first(r["partial"], 1)
    gather_forward(11)
    fold_next(r["partial"], 1)
    gather_forward(12)
    fold_last(1)

    def two_rows(group):
        rows_now = r["hidden_one"][group] + folded(r["partial"], 1, group)
        r["hidden_two"][group] = rows_now
        shaped, _ = norm_parts(rows_now)
        r["normed_three"][group, mine(spot), :] = (shaped * gain(GAIN_MLP)).astype(bf16)

    loop(groups, two_rows)
    spread_first(r["normed_three"], 2)
    gather_forward(13)
    spread_next(r["normed_three"], 2)
    spread_last(r["normed_three"], 2)

    def up_rows(index, at):
        pre = dot(flat(r["normed_three"][tile(index)]), full_w[UP + at])
        r["pre"][tile(index), :, at * width : (at + 1) * width] = pre.reshape(pairs, -1, width)
        r["act"][tile(index), :, at * width : (at + 1) * width] = (
            (pre * gelu_parts(pre)).astype(bf16).reshape(pairs, -1, width)
        )

    for at in range(downs):
        have_weights(UP + at)
        loop(tiles, functools.partial(up_rows, at=at))
    for chunk in range(14, chunks):
        gather_forward(chunk)

    spread_last(r["spread_out"], 3)

    def down_rows(index, at):
        back = dot(flat(r["spread_out"][tile(index)]), full_w[down + at])
        pre = flat(r["pre"][tile(index), :, at * width : (at + 1) * width])
        r["grad_pre"][tile(index), :, at * width : (at + 1) * width] = (
            (back * gelu_slope(pre)).astype(bf16).reshape(pairs, -1, width)
        )

    for at in range(downs):
        have_weights(down + at)
        loop(tiles, functools.partial(down_rows, at=at))
    fold_sent(1)
    project_back(r["partial"], [(r["grad_pre"], at * width, UP + at) for at in range(downs)])
    fold_first(r["partial"], 2)
    for at in range(downs):
        weight_grad(down + at, r["spread_out"], r["act"], at * width)
        if at == 0:
            fold_next(r["partial"], 2)
    fold_last(2)

    def back_two(group):
        grad = folded(r["partial"], 2, group)
        value = cot[group].astype(f32) + norm_back(r["hidden_two"][group], GAIN_MLP, grad)
        r["grad_two"][group] = value
        r["spread_two"][group, mine(spot), :] = value.astype(bf16)

    loop(groups, back_two)
    spread_first(r["spread_two"], 4)
    project_back(
        r["partial_out"], [(r["act"], at * width, down + at) for at in range(downs)]
    )
    fold_first(r["partial_out"], 3)
    weight_grad(UP, r["normed_three"], r["grad_pre"], 0)
    spread_next(r["spread_two"], 4)
    for at in range(1, downs):
        weight_grad(UP + at, r["normed_three"], r["grad_pre"], at * width)
    fold_next(r["partial_out"], 3)
    scatter_line(down)
    spread_last(r["spread_two"], 4)
    project(r["grad_att"], r["spread_two"], OS)

    def self_back(group):
        attend_back(
            group,
            r["q_two"],
            r["k_two"],
            0,
            r["v_two"],
            0,
            r["prob_two"],
            r["grad_att"],
            (r["gq_two"], r["gk_two"], 0, r["gv_two"], 0),
        )

    loop(groups, self_back)
    fold_sent(2)
    project_back(
        r["partial"],
        [(r["gq_two"], 0, QS), (r["gk_two"], 0, KS), (r["gv_two"], 0, VS)],
    )
    fold_first(r["partial"], 4)
    scatter_line(down + 1)
    weight_grad(OS, r["spread_two"], r["o_two"])
    fold_next(r["partial"], 4)
    weight_grad(QS, r["normed_two"], r["gq_two"])
    weight_grad(KS, r["normed_two"], r["gk_two"])
    weight_grad(VS, r["normed_two"], r["gv_two"])
    scatter_line(down + 2)
    fold_last(4)

    def back_one(group):
        grad = folded(r["partial"], 4, group)
        value = r["grad_two"][group] + norm_back(r["hidden_one"][group], GAIN_SELF, grad)
        r["grad_one"][group] = value
        r["spread_one"][group, mine(spot), :] = value.astype(bf16)

    loop(groups, back_one)
    spread_first(r["spread_one"], 5)
    scatter_line(down + 3)
    fold_last(3)

    def out_rows(group):
        r["block_out"][group] = (
            r["hidden_two"][group] + folded(r["partial_out"], 3, group)
        ).astype(bf16)

    loop(groups, out_rows)
    spread_next(r["spread_one"], 5)
    scatter_line(UP)
    spread_last(r["spread_one"], 5)
    project(r["grad_att"], r["spread_one"], OC)

    def cross_back(group):
        attend_back(
            group,
            r["q_one"],
            keys,
            0,
            keys,
            width,
            r["prob_one"],
            r["grad_att"],
            (r["gq_one"], r["grad_keys"], 0, r["grad_keys"], width),
        )

    loop(groups, cross_back)
    weight_grad(OC, r["spread_one"], r["o_one"])
    weight_grad(KC, normed_in, r["grad_keys"], 0)
    scatter_line(UP + 1)
    weight_grad(VC, normed_in, r["grad_keys"], width)
    weight_grad(QC, r["normed_lat"], r["gq_one"])
    fold_sent(4)
    project_back(r["partial"], [(r["gq_one"], 0, QC)])
    fold_first(r["partial"], 5)
    scatter_line(UP + 2)
    for group in range(groups):
        in_sent(group)

    def in_back(group):
        for piece in range(keys.shape[1] // 256):
            at = slice(piece * 256, piece * 256 + 256)

            def one(index):
                value = dot_t(
                    r["grad_keys"][group, at, :width], full_w[KC, lanes(index), :]
                ) + dot_t(r["grad_keys"][group, at, width:], full_w[VC, lanes(index), :])
                normed_in[group, at, lanes(index)] = value.astype(bf16)

            loop(depth // width, one)
        in_fold_first(group)

    loop(groups, in_back)
    scatter_line(UP + 3)
    fold_next(r["partial"], 5)
    loop(groups, in_fold_next)
    for chunk in (OS, QS, KS, VS):
        scatter_line(chunk)
    fold_last(5)

    def lat_back(group):
        grad = folded(r["partial"], 5, group)
        r["grad_lat"][group] = r["grad_one"][group] + norm_back(
            lat[group].astype(f32), GAIN_CROSS, grad
        )

    loop(groups, lat_back)

    def in_final(group):
        drain(in_row.at[group], in_fold_sems.at[group, 3])
        near = normed_in[group, mine_in(spot), :].astype(f32) + in_core[group, 0].astype(f32)
        grad = near + in_row[group].astype(f32)
        r["grad_in"][group] = norm_back(inp[group].astype(f32), GAIN_INPUT, grad)

    loop(groups, in_final)
    gain_sems, gain_sum, gain_recv = r["gain_sems"], r["gain_sum"], r["gain_recv"]
    gain_line = r["gain_line"]

    def gain_stage(stage, place):
        push(
            gain_sum.at[stage],
            gain_recv.at[stage],
            gain_sems.at[0, stage],
            gain_sems.at[1, stage],
            place,
        )

    def gain_got(stage):
        drain(gain_recv.at[stage], gain_sems.at[1, stage])
        return gain_sum[stage] + gain_recv[stage]

    gain_sum[0] = gain_mine[...]
    gain_stage(0, to_core)
    scatter_line(OC)
    gain_sum[1] = gain_got(0)
    gain_stage(1, to_row)
    scatter_line(KC)
    gain_sum[2] = gain_got(1)
    gain_stage(2, partner)
    scatter_line(VC)
    gain_line[row] = gain_got(2)

    def gain_send(step, carry):
        push(
            gain_line.at[row],
            gain_line.at[row],
            gain_sems.at[0, 3],
            gain_sems.at[1, 3],
            member(line_peer(step)),
        )
        return carry

    lax.fori_loop(1, line, gain_send, 0)
    scatter_line(QC)
    for chunk in list(range(down, down + downs)) + list(range(UP, UP + downs)):
        scatter_end(chunk)
    for chunk in (OS, QS, KS, VS, OC, KC, VC, QC):
        scatter_end(chunk)
    drain(gain_line.at[pl.ds(0, line - 1)], gain_sems.at[1, 3])
    whole = gain_line[0]
    for other in range(1, line):
        whole = whole + gain_line[other]
    r["grad_gain"][...] = whole

    def sent(chunk):
        drain(full_w.at[chunk, pl.ds(0, (line - 1) * rows), :], gather_sems.at[0, chunk])
        drain(full_w.at[chunk, pl.ds(0, line * rows), :], gather_sems.at[2, chunk])
        drain(pair_buf.at[chunk], scatter_sems.at[0, chunk])
        drain(line_buf.at[chunk], scatter_sems.at[2, chunk])

    loop(chunks, sent)
    for use, name in enumerate(
        ("normed_lat", "normed_two", "normed_three", "spread_out", "spread_two", "spread_one")
    ):
        spread_sent(r[name], use)
    fold_sent(3)
    fold_sent(5)

    def in_folds_sent(group):
        drain(in_core.at[group], in_fold_sems.at[group, 0])
        drain(in_row.at[group], in_fold_sems.at[group, 2])

    loop(groups, in_folds_sent)
    for stage in range(3):
        drain(gain_recv.at[stage], gain_sems.at[0, stage])
    drain(gain_line.at[pl.ds(0, line - 1)], gain_sems.at[0, 3])


def run_block(members, lat, inp, cot, allow, gains, shard):
    groups, own_lat, depth = lat.shape
    own_in = inp.shape[1]
    chunks, rows, width = shard.shape
    spots = allow.shape[2] // own_in
    latents, ins = own_lat * spots, own_in * spots
    hidden = (chunks - UP) // 2 * width
    line = members // PAIR
    heads = width // HEAD_DIM
    vmem = pltpu.VMEM
    vspec = pl.BlockSpec(memory_space=pltpu.VMEM)
    narrow = vmem((groups, latents, width), bf16)
    full = vmem((groups, latents, depth), bf16)
    own = vmem((groups, own_lat, depth), f32)
    dma = pltpu.SemaphoreType.DMA
    return pl.pallas_call(
        functools.partial(block_kernel, members),
        out_shape=(
            jax.ShapeDtypeStruct((groups, own_lat, depth), bf16),
            jax.ShapeDtypeStruct((groups, own_lat, depth), f32),
            jax.ShapeDtypeStruct((groups, own_in, depth), f32),
            jax.ShapeDtypeStruct(gains.shape, f32),
            jax.ShapeDtypeStruct(shard.shape, f32),
        ),
        in_specs=[vspec] * 5 + [pl.BlockSpec(memory_space=pl.ANY)],
        out_specs=(vspec,) * 5,
        scratch_shapes=[
            vmem((chunks, depth, width), bf16),
            vmem((chunks, depth, width), bf16),
            vmem((chunks, line * rows, width), bf16),
            vmem((chunks, (line - 1) * rows, width), bf16),
            vmem((groups, ins, depth), bf16),
            full,
            full,
            full,
            vmem((groups, ins, 2 * width), bf16),
            vmem((groups, ins, 2 * width), bf16),
        ]
        + [narrow] * 11
        + [
            vmem((groups, heads, latents, ins), f32),
            vmem((groups, heads, latents, latents), f32),
            vmem((groups, latents, hidden), f32),
            vmem((groups, latents, hidden), bf16),
            vmem((groups, latents, hidden), bf16),
            full,
            full,
            full,
            own,
            own,
            own,
            own,
            full,
            full,
            vmem((3, 2, groups, own_lat, depth), bf16),
            vmem((3, groups, own_lat, depth), bf16),
            vmem((groups, 2, own_in, depth), bf16),
            vmem((groups, own_in, depth), bf16),
            vmem(gains.shape, f32),
            vmem((3,) + gains.shape, f32),
            vmem((3,) + gains.shape, f32),
            vmem((line,) + gains.shape, f32),
            dma,
            dma((4, chunks)),
            dma((4, chunks)),
            dma((6, 6)),
            dma((6, 4)),
            dma((groups, 6)),
            dma((groups, 4)),
            dma((2, 4)),
        ],
        compiler_params=pltpu.CompilerParams(
            collective_id=0, has_side_effects=True, vmem_limit_bytes=VMEM_TOP
        ),
    )(lat, inp, cot, allow, gains, shard)


def to_chunks(matrix):
    rows, width = matrix.shape
    return matrix.reshape(rows, width // CHUNK, CHUNK).transpose(1, 0, 2)


def from_chunks(chunked):
    return chunked.transpose(1, 0, 2).reshape(chunked.shape[1], -1)


TURNED = (3, 7, 9)


def per_device(members, *args):
    (latents, inputs, input_masks, valid_counts) = args[:4]
    gain_set, weights, out_cotangent = args[4:8], args[8:18], args[18]
    by_rows = [w.T if index in TURNED else w for index, w in enumerate(weights)]
    widths = [weight.shape[1] for weight in by_rows]
    shard = to_chunks(jnp.concatenate(by_rows, axis=1))
    positions = jnp.arange(input_masks.shape[1], dtype=jnp.int32)
    allowed = (positions[None, :] < valid_counts[:, None]) & (
        (input_masks == 1) | (positions[None, :] == 0)
    )
    gains = jnp.concatenate([jnp.stack(gain_set), jnp.zeros((4, latents.shape[2]), f32)])
    block_out, grad_lat, grad_in, grad_gain, grad_w = run_block(
        members, latents, inputs, out_cotangent, allowed.astype(f32)[:, None, :], gains, shard
    )
    grads = []
    first = 0
    for index, width in enumerate(widths):
        grad = from_chunks(grad_w[first : first + width // CHUNK])
        grads.append(grad.T if index in TURNED else grad)
        first += width // CHUNK
    return (
        block_out,
        grad_lat,
        grad_in,
        grad_gain[0],
        grad_gain[1],
        grad_gain[2],
        grad_gain[3],
        *grads,
    )


def solution(mesh):
    rows_first = P("dp", "head")
    cols_first = P("head", "dp")
    tokens = P("dp", "head", None)
    weight_specs = tuple(cols_first if index in TURNED else rows_first for index in range(10))
    in_specs = (tokens, tokens, P("dp", None), P("dp"), P(), P(), P(), P(), *weight_specs, tokens)
    out_specs = (tokens, tokens, tokens, P(), P(), P(), P(), *weight_specs)
    return jax.shard_map(
        functools.partial(per_device, mesh.shape["dp"]),
        mesh=mesh,
        in_specs=in_specs,
        out_specs=out_specs,
        check_vma=False,
    )
```

```python
import functools
import typing

import jax
import jax.numpy as jnp
from jax import lax
from jax.experimental import pallas as pl
from jax.experimental.pallas import tpu as pltpu
from jax.sharding import PartitionSpec as P

HEAD_DIM = 128
CHUNK = 256
PAIR = 2
CORES = 2
MESH = pl.DeviceIdType.MESH
VMEM_TOP = 64 * 1024 * 1024 - 64 * 1024

QC, KC, VC, OC, QS, KS, VS, OS, UP = 0, 1, 2, 3, 4, 5, 6, 7, 8

FOLD_SLOT = (0, 1, 0, 1, 0, 0)

bf16 = jnp.bfloat16
f32 = jnp.float32
epsilon = 1e-05


def dot(left, right):
    return lax.dot_general(left, right, (((1,), (0,)), ((), ())), preferred_element_type=f32)


def dot_t(left, right):
    return lax.dot_general(left, right, (((1,), (1,)), ((), ())), preferred_element_type=f32)


def t_dot(left, right):
    return lax.dot_general(left, right, (((0,), (0,)), ((), ())), preferred_element_type=f32)


def norm_parts(rows):
    centered = rows - jnp.mean(rows, axis=-1, keepdims=True)
    scale = lax.rsqrt(jnp.mean(centered * centered, axis=-1, keepdims=True) + epsilon)
    return centered * scale, scale


def gelu_parts(pre):
    bend = 0.7978845608028654 * (pre + 0.044715 * pre * pre * pre)
    return 0.5 * (1.0 + jnp.tanh(bend))


def gelu_slope(pre):
    squared = pre * pre
    tanh = jnp.tanh(0.7978845608028654 * (pre + 0.044715 * pre * squared))
    inner = 0.7978845608028654 * (1.0 + 3 * 0.044715 * squared)
    return 0.5 * (1.0 + tanh) + 0.5 * pre * (1.0 - tanh * tanh) * inner


def loop(count, body):
    def step(index, carry):
        body(index)
        return carry

    lax.fori_loop(0, count, step, 0)


def flat(value):
    return value.reshape(-1, value.shape[-1])


def push(source, target, send_sem, recv_sem, place):
    pltpu.make_async_remote_copy(
        src_ref=source,
        dst_ref=target,
        send_sem=send_sem,
        recv_sem=recv_sem,
        device_id=place,
        device_id_type=MESH,
    ).start()


def drain(like, sem):
    pltpu.make_async_copy(like, like, sem).wait()


class Refs(typing.NamedTuple):
    lat: typing.Any
    inp: typing.Any
    cot: typing.Any
    mask: typing.Any
    counts: typing.Any
    gain_input: typing.Any
    gain_cross: typing.Any
    gain_self: typing.Any
    gain_mlp: typing.Any
    query_cross: typing.Any
    key_cross: typing.Any
    value_cross: typing.Any
    output_cross: typing.Any
    query_self: typing.Any
    key_self: typing.Any
    value_self: typing.Any
    output_self: typing.Any
    mlp_up: typing.Any
    mlp_down: typing.Any
    block_out: typing.Any
    grad_lat: typing.Any
    grad_in: typing.Any
    grad_gain: typing.Any
    grad_w: typing.Any
    allow: typing.Any
    full_w: typing.Any
    part_w: typing.Any
    pair_buf: typing.Any
    line_buf: typing.Any
    normed_in: typing.Any
    normed_lat: typing.Any
    normed_two: typing.Any
    normed_three: typing.Any
    keys: typing.Any
    grad_keys: typing.Any
    q_one: typing.Any
    o_one: typing.Any
    q_two: typing.Any
    k_two: typing.Any
    v_two: typing.Any
    o_two: typing.Any
    gq_one: typing.Any
    gq_two: typing.Any
    gk_two: typing.Any
    gv_two: typing.Any
    grad_att: typing.Any
    prob_one: typing.Any
    prob_two: typing.Any
    pre: typing.Any
    act: typing.Any
    grad_pre: typing.Any
    spread_out: typing.Any
    spread_two: typing.Any
    spread_one: typing.Any
    hidden_one: typing.Any
    hidden_two: typing.Any
    grad_two: typing.Any
    grad_one: typing.Any
    partial: typing.Any
    partial_out: typing.Any
    fold_core: typing.Any
    fold_row: typing.Any
    in_core: typing.Any
    in_row: typing.Any
    gain_mine: typing.Any
    gain_sum: typing.Any
    gain_recv: typing.Any
    gain_line: typing.Any
    own_sem: typing.Any
    gather_sems: typing.Any
    scatter_sems: typing.Any
    spread_sems: typing.Any
    fold_sems: typing.Any
    in_sems: typing.Any
    in_fold_sems: typing.Any
    relay_sems: typing.Any
    gain_sems: typing.Any


def block_kernel(members, turned, *refs):
    r = Refs(*refs)
    groups, own_lat, depth = r.lat.shape
    own_in = r.inp.shape[1]
    hidden = r.act.shape[2]
    chunks, rows, width = r.grad_w.shape
    heads = width // HEAD_DIM
    downs = hidden // width
    down = UP + downs
    scaling = HEAD_DIM ** (-0.5)
    pairs = 2 if groups % 2 == 0 else 1
    tiles = groups // pairs

    me = lax.axis_index("dp")
    line = members // PAIR
    row, column = me // PAIR, me % PAIR
    partner = {"dp": row * PAIR + 1 - column}
    spot = lax.axis_index("head")
    side, core = spot // CORES, spot % CORES
    spot_core = side * CORES + 1 - core
    spot_row = (1 - side) * CORES + core
    spot_both = (1 - side) * CORES + 1 - core
    to_core = {"head": spot_core}
    to_row = {"head": spot_row}

    def line_peer(step):
        return lax.rem(row + step, line)

    def member(other):
        return {"dp": other * PAIR + column}

    barrier = pltpu.get_barrier_semaphore()
    for place in (partner, to_core, to_row):
        pl.semaphore_signal(barrier, inc=1, device_id=place, device_id_type=MESH)

    def hello(step, carry):
        pl.semaphore_signal(
            barrier, inc=1, device_id=member(line_peer(step)), device_id_type=MESH
        )
        return carry

    lax.fori_loop(1, line, hello, 0)
    pl.semaphore_wait(barrier, line + 2)

    full_w, part_w = r.full_w, r.part_w
    gather_sems, scatter_sems = r.gather_sems, r.scatter_sems

    downs_from = chunks - (chunks - UP) // 2

    def holder(chunk):
        if chunk >= downs_from:
            return r.mlp_down, chunk - downs_from
        if chunk >= UP:
            return r.mlp_up, chunk - UP
        whole = (
            r.query_cross,
            r.key_cross,
            r.value_cross,
            r.output_cross,
            r.query_self,
            r.key_self,
            r.value_self,
            r.output_self,
        )
        return whole[chunk], 0

    def shard(chunk):
        weight, piece = holder(chunk)
        if chunk in turned:
            return block(chunk, me)
        return weight.at[:, piece * width : (piece + 1) * width]

    def block(chunk, other):
        return full_w.at[chunk, pl.ds(pl.multiple_of(other * rows, rows), rows), :]

    hops = line - 1 if line <= 4 else 1
    relayed = line <= 4
    twice = (7, 13) if relayed else ()
    relay_sems = r.relay_sems
    ticks = [0]

    def span(chunk, other):
        if chunk in twice:
            first = pl.multiple_of(other * PAIR * rows, PAIR * rows)
            return full_w.at[chunk, pl.ds(first, PAIR * rows), :]
        return block(chunk, other * PAIR + column)

    def gather_direct(chunk):
        def one(step, carry):
            push(
                shard(chunk),
                block(chunk, me),
                gather_sems.at[0, chunk],
                gather_sems.at[1, chunk],
                member(line_peer(step)),
            )
            return carry

        lax.fori_loop(1, line, one, 0)

    def gather_pair(chunk):
        push(
            shard(chunk),
            block(chunk, me),
            gather_sems.at[2, chunk],
            gather_sems.at[3, chunk],
            partner,
        )

    def along(chunk, source, target, way, hop):
        @pl.when((row + way >= 0) & (row + way < line))
        def _():
            push(
                source,
                target,
                gather_sems.at[0, chunk],
                relay_sems.at[chunk, (1 - way) // 2, hop],
                member(row + way),
            )

    def gather_start(chunk):
        if not relayed:
            gather_direct(chunk)
            return
        source, target = shard(chunk), block(chunk, me)
        if chunk in twice:
            drain(target, gather_sems.at[3, chunk])
            source = target = span(chunk, row)
        for way in (1, -1):
            along(chunk, source, target, way, 0)

    def relay(chunk, hop):
        for way in (1, -1):
            other = row - way * hop

            @pl.when((other >= 0) & (other < line))
            def _():
                got = span(chunk, other)
                drain(got, relay_sems.at[chunk, (1 - way) // 2, hop - 1])
                if hop < line - 1:
                    along(chunk, got, got, way, hop)
                if chunk not in twice:
                    push(got, got, gather_sems.at[2, chunk], gather_sems.at[3, chunk], partner)

    def forward_direct(chunk):
        drain(full_w.at[chunk, pl.ds(0, (line - 1) * rows), :], gather_sems.at[1, chunk])

        def one(step, carry):
            source = block(chunk, line_peer(step) * PAIR + column)
            push(source, source, gather_sems.at[2, chunk], gather_sems.at[3, chunk], partner)
            return carry

        lax.fori_loop(1, line, one, 0)

    def tick():
        now = ticks[0]
        ticks[0] = now + 1
        for hop in range(1, hops + 1):
            if 0 <= now - hop + 1 < chunks:
                (relay if relayed else lambda chunk, _: forward_direct(chunk))(now - hop + 1, hop)
        if now + 2 < chunks:
            gather_start(now + 2)
        if now + ahead < chunks and now + ahead not in twice:
            gather_pair(now + ahead)

    def ticked(count):
        while ticks[0] < min(count, chunks + hops - 1):
            tick()

    def have_weights(chunk):
        ticked(chunk + hops)
        if chunk not in twice:
            drain(full_w.at[chunk, pl.ds(0, line * rows), :], gather_sems.at[3, chunk])

    def gather_sent(chunk):
        size = PAIR if chunk in twice else 1
        count = line - 1
        if relayed:
            count = jnp.where(row < line - 1, row + 1, 0) + jnp.where(row > 0, line - row, 0)
        like = full_w.at[chunk, pl.ds(0, size * rows), :]
        loop(count, lambda index: drain(like, gather_sems.at[0, chunk]))
        back = 1 if chunk in twice else line
        drain(full_w.at[chunk, pl.ds(0, back * rows), :], gather_sems.at[2, chunk])

    ahead = min(3, chunks)

    def part(index):
        return pl.ds(pl.multiple_of(index * rows, rows), rows)

    pair_buf, line_buf, total = r.pair_buf, r.line_buf, r.grad_w

    def scatter_pair(chunk):
        def one(other):
            push(
                part_w.at[chunk, part(other * PAIR + 1 - column), :],
                pair_buf.at[chunk, part(other), :],
                scatter_sems.at[0, chunk],
                scatter_sems.at[1, chunk],
                partner,
            )

        loop(line, one)

    def scatter_line(chunk):
        drain(pair_buf.at[chunk], scatter_sems.at[1, chunk])
        own = part_w[chunk, part(me), :].astype(f32)
        total[chunk] = own + pair_buf[chunk, part(row), :].astype(f32)

        def one(step, carry):
            other = line_peer(step)
            mine = part_w[chunk, part(other * PAIR + column), :].astype(f32)
            theirs = pair_buf[chunk, part(other), :].astype(f32)
            pair_buf[chunk, part(other), :] = (mine + theirs).astype(bf16)
            push(
                pair_buf.at[chunk, part(other), :],
                line_buf.at[chunk, part(step - 1), :],
                scatter_sems.at[2, chunk],
                scatter_sems.at[3, chunk],
                member(other),
            )
            return carry

        lax.fori_loop(1, line, one, 0)

    def scatter_end(chunk):
        drain(line_buf.at[chunk], scatter_sems.at[3, chunk])

        def one(step, carry):
            total[chunk] += line_buf[chunk, part(step - 1), :].astype(f32)
            return carry

        lax.fori_loop(1, line, one, 0)

    spread_sems, fold_sems = r.spread_sems, r.fold_sems

    def mine(spot_at):
        return pl.ds(pl.multiple_of(spot_at * own_lat, own_lat), own_lat)

    def mine_in(spot_at):
        return pl.ds(pl.multiple_of(spot_at * own_in, own_in), own_in)

    def some(half):
        return pl.ds(half * pairs, pairs)

    def slot(use, half):
        return use * tiles + half

    def spread_first(full, use, half):
        own = full.at[some(half), mine(spot), :]
        at = slot(use, half)
        push(own, own, spread_sems.at[at, 0], spread_sems.at[at, 1], to_row)
        push(own, own, spread_sems.at[at, 2], spread_sems.at[at, 3], to_core)

    def spread_next(full, use, half):
        got = full.at[some(half), mine(spot_row), :]
        at = slot(use, half)
        drain(got, spread_sems.at[at, 1])
        push(got, got, spread_sems.at[at, 4], spread_sems.at[at, 5], to_core)

    def spread_last(full, use, half):
        like = full.at[some(half), mine(spot), :]
        drain(like, spread_sems.at[slot(use, half), 3])
        drain(like, spread_sems.at[slot(use, half), 5])

    def spread_sent(full, use, half):
        for which in (0, 2, 4):
            drain(full.at[some(half), mine(spot), :], spread_sems.at[slot(use, half), which])

    fold_core, fold_row = r.fold_core, r.fold_row

    def fold_first(whole, use, half):
        for place, spot_at in enumerate((spot_core, spot_both)):
            push(
                whole.at[some(half), mine(spot_at), :],
                fold_core.at[FOLD_SLOT[use], place, some(half)],
                fold_sems.at[slot(use, half), 0],
                fold_sems.at[slot(use, half), 1],
                to_core,
            )

    def fold_next(whole, use, half):
        drain(fold_core.at[FOLD_SLOT[use], :, some(half)], fold_sems.at[slot(use, half), 1])
        for group in range(half * pairs, half * pairs + pairs):
            near = whole[group, mine(spot_row), :].astype(f32)
            far = fold_core[FOLD_SLOT[use], 1, group].astype(f32)
            whole[group, mine(spot_row), :] = (near + far).astype(bf16)
        push(
            whole.at[some(half), mine(spot_row), :],
            fold_row.at[FOLD_SLOT[use], some(half)],
            fold_sems.at[slot(use, half), 2],
            fold_sems.at[slot(use, half), 3],
            to_row,
        )

    def fold_last(use, half):
        drain(fold_row.at[FOLD_SLOT[use], some(half)], fold_sems.at[slot(use, half), 3])

    def folded(whole, use, group):
        near = whole[group, mine(spot), :].astype(f32) + fold_core[FOLD_SLOT[use], 0, group].astype(f32)
        return near + fold_row[FOLD_SLOT[use], group].astype(f32)

    def fold_sent(use, half):
        drain(fold_core.at[FOLD_SLOT[use], :, some(half)], fold_sems.at[slot(use, half), 0])
        drain(fold_row.at[FOLD_SLOT[use], some(half)], fold_sems.at[slot(use, half), 2])

    in_sems, in_fold_sems = r.in_sems, r.in_fold_sems
    normed_in = r.normed_in

    def in_first(group):
        own = normed_in.at[group, mine_in(spot), :]
        push(own, own, in_sems.at[group, 0], in_sems.at[group, 1], to_row)
        push(own, own, in_sems.at[group, 2], in_sems.at[group, 3], to_core)

    def in_next(group):
        got = normed_in.at[group, mine_in(spot_row), :]
        drain(got, in_sems.at[group, 1])
        push(got, got, in_sems.at[group, 4], in_sems.at[group, 5], to_core)

    def in_last(group):
        like = normed_in.at[group, mine_in(spot), :]
        drain(like, in_sems.at[group, 3])
        drain(like, in_sems.at[group, 5])

    def in_sent(group):
        for which in (0, 2, 4):
            drain(normed_in.at[group, mine_in(spot), :], in_sems.at[group, which])

    in_core, in_row = r.in_core, r.in_row
    ins = normed_in.shape[1]
    blocks, stacked = depth // width, depth // ins

    def dn_in(group, piece, at):
        first = piece % stacked * ins
        if not isinstance(piece, int):
            first = pl.multiple_of(first, ins)
        index = UP + (group * blocks + piece) // stacked
        return full_w.at[index, pl.ds(first + at.start, at.size), :]

    def in_fold_first(group):
        for place, spot_at in enumerate((spot_core, spot_both)):
            for piece in range(blocks):
                push(
                    dn_in(group, piece, mine_in(spot_at)),
                    in_core.at[group, place, piece],
                    in_fold_sems.at[group, 0],
                    in_fold_sems.at[group, 1],
                    to_core,
                )

    def in_fold_next(group):
        drain(in_core.at[group], in_fold_sems.at[group, 1])
        for piece in range(blocks):
            own = dn_in(group, piece, mine_in(spot_row))
            own[...] = (own[...].astype(f32) + in_core[group, 1, piece].astype(f32)).astype(bf16)
            push(
                own,
                in_row.at[group, piece],
                in_fold_sems.at[group, 2],
                in_fold_sems.at[group, 3],
                to_row,
            )

    lat, inp, cot = r.lat, r.inp, r.cot
    all_gains = (r.gain_input, r.gain_cross, r.gain_self, r.gain_mlp)

    def gain(index):
        return all_gains[index][...]

    def lanes(index, size=width):
        return pl.ds(pl.multiple_of(index * size, size), size)

    def project(target, source, chunk, half):
        value = dot(flat(source[some(half)]), full_w[chunk])
        target[some(half)] = value.astype(bf16).reshape(pairs, -1, width)

    def project_back(target, terms, half):
        def one(piece):
            value = None
            for source, first, chunk in terms:
                term = dot_t(
                    flat(source[some(half), :, first : first + width]),
                    full_w[chunk, lanes(piece), :],
                )
                value = term if value is None else value + term
            target[some(half), :, lanes(piece)] = value.astype(bf16).reshape(pairs, -1, width)

        loop(blocks, one)

    def weight_grad(chunk, left, right, first=0, send=True):
        def one(index):
            value = None
            for group in range(0, groups, pairs):
                for_rows = pl.ds(group, pairs)
                term = t_dot(
                    flat(left[for_rows, :, lanes(index)]),
                    flat(right[for_rows, :, first : first + width]),
                )
                value = term if value is None else value + term
            part_w[chunk, lanes(index), :] = value.astype(bf16)

        loop(blocks, one)
        if send:
            scatter_pair(chunk)

    def each(half, body):
        loop(pairs, lambda index: body(half * pairs + index))

    def attend(group, queries, keys, key_at, values, value_at, prob, target, masked):
        for head in range(heads):
            at = head * HEAD_DIM
            query = queries[group, :, at : at + HEAD_DIM]
            key = keys[group, :, key_at + at : key_at + at + HEAD_DIM]
            value = values[group, :, value_at + at : value_at + at + HEAD_DIM]
            scores = dot_t(query, key) * scaling
            if masked:
                scores = jnp.where(r.allow[group] > 0.5, scores, -1e30)
            grown = jnp.exp(scores - jnp.max(scores, axis=-1, keepdims=True))
            share = grown / jnp.sum(grown, axis=-1, keepdims=True)
            prob[group, head] = share
            target[group, :, at : at + HEAD_DIM] = dot(share.astype(bf16), value).astype(bf16)

    def attend_back(group, queries, keys, key_at, values, value_at, prob, grad, outs):
        (gq, gk, gk_at, gv, gv_at) = outs
        for head in range(heads):
            at = head * HEAD_DIM
            query = queries[group, :, at : at + HEAD_DIM]
            key = keys[group, :, key_at + at : key_at + at + HEAD_DIM]
            value = values[group, :, value_at + at : value_at + at + HEAD_DIM]
            back = grad[group, :, at : at + HEAD_DIM]
            share = prob[group, head]
            slope = dot_t(back, value)
            slope = share * (slope - jnp.sum(share * slope, axis=-1, keepdims=True))
            slope = slope.astype(bf16)
            gq[group, :, at : at + HEAD_DIM] = (dot(slope, key) * scaling).astype(bf16)
            gk[group, :, gk_at + at : gk_at + at + HEAD_DIM] = (
                t_dot(slope, query) * scaling
            ).astype(bf16)
            gv[group, :, gv_at + at : gv_at + at + HEAD_DIM] = t_dot(
                share.astype(bf16), back
            ).astype(bf16)

    gain_mine = r.gain_mine
    gain_mine[...] = jnp.zeros_like(gain_mine)

    def norm_back(rows_in, index, grad):
        shaped, scale = norm_parts(rows_in)
        gain_mine[index : index + 1, :] += jnp.sum(grad * shaped, axis=0, keepdims=True)
        grad = grad * gain(index)
        center = jnp.mean(grad, axis=-1, keepdims=True)
        along = jnp.mean(grad * shaped, axis=-1, keepdims=True)
        return (grad - center - shaped * along) * scale

    GAIN_INPUT, GAIN_CROSS, GAIN_SELF, GAIN_MLP = 0, 1, 2, 3

    straight = [chunk for chunk in range(chunks) if chunk not in turned]
    for chunk in turned:
        weight, piece = holder(chunk)
        value = weight[piece * width : (piece + 1) * width, :].astype(f32)
        full_w[chunk, pl.ds(pl.multiple_of(me * rows, rows), rows), :] = value.T.astype(bf16)
    for chunk in straight:
        pltpu.make_async_copy(shard(chunk), block(chunk, me), r.own_sem).start()
    for chunk in range(chunks):
        if chunk < ahead or chunk in twice:
            gather_pair(chunk)
    for chunk in range(min(2, chunks)):
        gather_start(chunk)
    halves = range(tiles)

    def lat_rows(group):
        shaped, _ = norm_parts(lat[group].astype(f32))
        r.normed_lat[group, mine(spot), :] = (shaped * gain(GAIN_CROSS)).astype(bf16)

    for half in halves:
        each(half, lat_rows)
        spread_first(r.normed_lat, 0, half)

    def in_rows(group):
        shaped, _ = norm_parts(inp[group].astype(f32))
        normed_in[group, mine_in(spot), :] = (shaped * gain(GAIN_INPUT)).astype(bf16)
        in_first(group)

    loop(groups, in_rows)
    r.spread_out[:, mine(spot), :] = cot[...]
    for half in halves:
        spread_first(r.spread_out, 3, half)
    ticked(1)
    for half in halves:
        spread_next(r.normed_lat, 0, half)
    ticked(2)
    in_next(0)
    ticked(3)
    if groups > 1:
        in_next(1)
    drain(full_w.at[pl.ds(0, len(straight)), pl.ds(0, rows), :], r.own_sem)
    positions = lax.broadcasted_iota(jnp.int32, (1, ins), 1)
    for group in range(groups):
        allowed = (positions < r.counts[group]) & (
            (r.mask[group : group + 1, :] == 1) | (positions == 0)
        )
        r.allow[group] = allowed.astype(f32)
    have_weights(QC)
    for half in halves:
        spread_last(r.normed_lat, 0, half)
        project(r.q_one, r.normed_lat, QC, half)
    have_weights(KC)
    if groups > 2:
        in_next(2)
    have_weights(VC)
    keys = r.keys
    piece_rows = min(256, ins)

    def key_rows(group):
        in_last(group)
        for piece in range(ins // piece_rows):
            at = slice(piece * piece_rows, piece * piece_rows + piece_rows)
            keys[group, at, :width] = dot(normed_in[group, at, :], full_w[KC]).astype(bf16)
            keys[group, at, width:] = dot(normed_in[group, at, :], full_w[VC]).astype(bf16)
        attend(group, r.q_one, keys, 0, keys, width, r.prob_one, r.o_one, True)

    each(0, key_rows)
    for group in range(3, groups):
        in_next(group)
    have_weights(OC)
    project_back(r.partial, [(r.o_one, 0, OC)], 0)
    fold_first(r.partial, 0, 0)
    for half in halves[1:]:
        each(half, key_rows)
        fold_next(r.partial, 0, half - 1)
        project_back(r.partial, [(r.o_one, 0, OC)], half)
        fold_first(r.partial, 0, half)
    ticked(7)
    fold_next(r.partial, 0, tiles - 1)
    for half in halves:
        spread_next(r.spread_out, 3, half)
    ticked(8)

    def one_rows(group):
        rows_now = lat[group].astype(f32) + folded(r.partial, 0, group)
        r.hidden_one[group] = rows_now
        shaped, _ = norm_parts(rows_now)
        r.normed_two[group, mine(spot), :] = (shaped * gain(GAIN_SELF)).astype(bf16)

    for half in halves:
        fold_last(0, half)
        each(half, one_rows)
        spread_first(r.normed_two, 1, half)
    for half in halves:
        spread_next(r.normed_two, 1, half)
    have_weights(QS)
    have_weights(KS)
    have_weights(VS)

    def self_rows(group):
        attend(group, r.q_two, r.k_two, 0, r.v_two, 0, r.prob_two, r.o_two, False)

    for half in halves:
        spread_last(r.normed_two, 1, half)
        for target, chunk in ((r.q_two, QS), (r.k_two, KS), (r.v_two, VS)):
            project(target, r.normed_two, chunk, half)
        each(half, self_rows)
        if half == 0:
            have_weights(OS)
        fold_sent(0, half)
        project_back(r.partial, [(r.o_two, 0, OS)], half)
        fold_first(r.partial, 1, half)
        if half > 0:
            fold_next(r.partial, 1, half - 1)
    ticked(11)
    fold_next(r.partial, 1, tiles - 1)

    def two_rows(group):
        rows_now = r.hidden_one[group] + folded(r.partial, 1, group)
        r.hidden_two[group] = rows_now
        shaped, _ = norm_parts(rows_now)
        r.normed_three[group, mine(spot), :] = (shaped * gain(GAIN_MLP)).astype(bf16)

    for half in halves:
        fold_last(1, half)
        each(half, two_rows)
        spread_first(r.normed_three, 2, half)
    ticked(12)
    for half in halves:
        spread_next(r.normed_three, 2, half)
    ticked(13)

    def up_rows(half, at):
        pre = dot(flat(r.normed_three[some(half)]), full_w[UP + at])
        r.pre[some(half), :, at * width : (at + 1) * width] = pre.reshape(pairs, -1, width)
        r.act[some(half), :, at * width : (at + 1) * width] = (
            (pre * gelu_parts(pre)).astype(bf16).reshape(pairs, -1, width)
        )

    for half in halves:
        spread_last(r.normed_three, 2, half)
        spread_last(r.spread_out, 3, half)
    for at in range(downs):
        have_weights(UP + at)
        for half in halves:
            up_rows(half, at)
        weight_grad(down + at, r.spread_out, r.act, at * width, send=False)

    def down_rows(half, at):
        back = dot(flat(r.spread_out[some(half)]), full_w[down + at])
        pre = flat(r.pre[some(half), :, at * width : (at + 1) * width])
        r.grad_pre[some(half), :, at * width : (at + 1) * width] = (
            (back * gelu_slope(pre)).astype(bf16).reshape(pairs, -1, width)
        )

    for at in range(downs):
        have_weights(down + at)
        if at == downs - 1:
            for other in range(downs):
                scatter_pair(down + other)
        for half in halves:
            down_rows(half, at)
        if at < downs - 1:
            weight_grad(UP + at, r.normed_three, r.grad_pre, at * width, send=False)
    for half in halves:
        fold_sent(1, half)
        project_back(
            r.partial, [(r.grad_pre, at * width, UP + at) for at in range(downs)], half
        )
        fold_first(r.partial, 2, half)
    for at in range(downs - 1):
        scatter_pair(UP + at)
    weight_grad(UP + downs - 1, r.normed_three, r.grad_pre, (downs - 1) * width)
    for half in halves:
        fold_next(r.partial, 2, half)
    for half in halves:
        project_back(
            r.partial_out, [(r.act, at * width, down + at) for at in range(downs)], half
        )
        fold_first(r.partial_out, 3, half)

    def back_two(group):
        grad = folded(r.partial, 2, group)
        value = cot[group].astype(f32) + norm_back(r.hidden_two[group], GAIN_MLP, grad)
        r.grad_two[group] = value
        r.spread_two[group, mine(spot), :] = value.astype(bf16)

    for half in halves:
        fold_last(2, half)
        each(half, back_two)
        spread_first(r.spread_two, 4, half)
    scatter_line(down)
    for half in halves:
        spread_next(r.spread_two, 4, half)
    scatter_line(down + 1)
    for half in halves:
        fold_next(r.partial_out, 3, half)

    def self_back(group):
        attend_back(
            group,
            r.q_two,
            r.k_two,
            0,
            r.v_two,
            0,
            r.prob_two,
            r.grad_att,
            (r.gq_two, r.gk_two, 0, r.gv_two, 0),
        )

    for half in halves:
        spread_last(r.spread_two, 4, half)
        project(r.grad_att, r.spread_two, OS, half)
        each(half, self_back)
        fold_sent(2, half)
        project_back(
            r.partial, [(r.gq_two, 0, QS), (r.gk_two, 0, KS), (r.gv_two, 0, VS)], half
        )
        fold_first(r.partial, 4, half)
        if half > 0:
            fold_next(r.partial, 4, half - 1)
    scatter_line(down + 2)
    weight_grad(OS, r.spread_two, r.o_two)
    fold_next(r.partial, 4, tiles - 1)
    weight_grad(QS, r.normed_two, r.gq_two)
    weight_grad(KS, r.normed_two, r.gk_two)

    def back_one(group):
        grad = folded(r.partial, 4, group)
        value = r.grad_two[group] + norm_back(r.hidden_one[group], GAIN_SELF, grad)
        r.grad_one[group] = value
        r.spread_one[group, mine(spot), :] = value.astype(bf16)

    for half in halves:
        fold_last(4, half)
        each(half, back_one)
        spread_first(r.spread_one, 5, half)
    scatter_line(down + 3)
    weight_grad(VS, r.normed_two, r.gv_two)
    for half in halves:
        spread_next(r.spread_one, 5, half)
    scatter_line(UP)

    def out_rows(group):
        r.block_out[group] = (
            r.hidden_two[group] + folded(r.partial_out, 3, group)
        ).astype(bf16)

    for chunk in range(chunks):
        gather_sent(chunk)

    def cross_back(group):
        attend_back(
            group,
            r.q_one,
            keys,
            0,
            keys,
            width,
            r.prob_one,
            r.grad_att,
            (r.gq_one, r.grad_keys, 0, r.grad_keys, width),
        )

    def in_back(group):
        for at in range(0, ins, piece_rows):

            def one(piece):
                value = dot_t(
                    r.grad_keys[group, at : at + piece_rows, :width], full_w[KC, lanes(piece), :]
                ) + dot_t(
                    r.grad_keys[group, at : at + piece_rows, width:], full_w[VC, lanes(piece), :]
                )
                dn_in(group, piece, pl.ds(at, piece_rows))[...] = value.astype(bf16)

            loop(blocks, one)
        in_fold_first(group)

    for half in halves:
        spread_last(r.spread_one, 5, half)
        project(r.grad_att, r.spread_one, OC, half)
        each(half, cross_back)
        each(half, in_back)
        if half == 0:
            scatter_line(UP + 1)
    weight_grad(OC, r.spread_one, r.o_one)
    for half in halves[:1]:
        each(half, in_fold_next)
    weight_grad(KC, normed_in, r.grad_keys, 0)
    scatter_line(UP + 2)
    for half in halves[1:]:
        each(half, in_fold_next)
    weight_grad(VC, normed_in, r.grad_keys, width)
    for half in halves:
        fold_sent(4, half)
        project_back(r.partial, [(r.gq_one, 0, QC)], half)
        fold_first(r.partial, 5, half)
    weight_grad(QC, r.normed_lat, r.gq_one)
    for half in halves:
        fold_next(r.partial, 5, half)
    scatter_line(UP + 3)
    for half in halves:
        fold_last(3, half)
        each(half, out_rows)
    for group in range(groups):
        in_sent(group)
    for chunk in (OS, QS):
        scatter_line(chunk)

    def in_final(group):
        drain(in_row.at[group], in_fold_sems.at[group, 3])
        parts = []
        for piece in range(blocks):
            near = dn_in(group, piece, mine_in(spot))[...].astype(f32)
            near = near + in_core[group, 0, piece].astype(f32)
            parts.append(near + in_row[group, piece].astype(f32))
        grad = jnp.concatenate(parts, axis=-1)
        r.grad_in[group] = norm_back(inp[group].astype(f32), GAIN_INPUT, grad)

    each(0, in_final)
    for chunk in (KS, VS):
        scatter_line(chunk)
    for half in halves[1:]:
        each(half, in_final)

    def lat_back(group):
        grad = folded(r.partial, 5, group)
        r.grad_lat[group] = r.grad_one[group] + norm_back(
            lat[group].astype(f32), GAIN_CROSS, grad
        )

    for half in halves:
        fold_last(5, half)
        each(half, lat_back)
    gain_sems, gain_sum, gain_recv = r.gain_sems, r.gain_sum, r.gain_recv
    gain_line = r.gain_line

    def gain_stage(stage, place):
        push(
            gain_sum.at[stage],
            gain_recv.at[stage],
            gain_sems.at[0, stage],
            gain_sems.at[1, stage],
            place,
        )

    def gain_got(stage):
        drain(gain_recv.at[stage], gain_sems.at[1, stage])
        return gain_sum[stage] + gain_recv[stage]

    gain_sum[0] = gain_mine[...]
    gain_stage(0, to_core)
    scatter_line(OC)
    gain_sum[1] = gain_got(0)
    gain_stage(1, to_row)
    scatter_line(KC)
    gain_sum[2] = gain_got(1)
    gain_stage(2, partner)
    scatter_line(VC)
    gain_line[row] = gain_got(2)

    def gain_send(step, carry):
        push(
            gain_line.at[row],
            gain_line.at[row],
            gain_sems.at[0, 3],
            gain_sems.at[1, 3],
            member(line_peer(step)),
        )
        return carry

    lax.fori_loop(1, line, gain_send, 0)
    scatter_line(QC)
    for chunk in list(range(down, down + downs)) + list(range(UP, UP + downs)):
        scatter_end(chunk)
    for chunk in (OS, QS, KS, VS, OC, KC, VC, QC):
        scatter_end(chunk)
    drain(gain_line.at[pl.ds(0, line - 1)], gain_sems.at[1, 3])
    whole = gain_line[0]
    for other in range(1, line):
        whole = whole + gain_line[other]
    r.grad_gain[...] = whole

    def sent(chunk):
        drain(pair_buf.at[chunk], scatter_sems.at[0, chunk])
        drain(line_buf.at[chunk], scatter_sems.at[2, chunk])

    loop(chunks, sent)
    spreads = (
        r.normed_lat,
        r.normed_two,
        r.normed_three,
        r.spread_out,
        r.spread_two,
        r.spread_one,
    )
    for use, full in enumerate(spreads):
        for half in halves:
            spread_sent(full, use, half)
    for half in halves:
        fold_sent(3, half)
        fold_sent(5, half)

    def in_folds_sent(group):
        drain(in_core.at[group], in_fold_sems.at[group, 0])
        drain(in_row.at[group], in_fold_sems.at[group, 2])

    loop(groups, in_folds_sent)
    for stage in range(3):
        drain(gain_recv.at[stage], gain_sems.at[0, stage])
    drain(gain_line.at[pl.ds(0, line - 1)], gain_sems.at[0, 3])


def run_block(members, turned, *args):
    lat, inp, cot, mask = args[:4]
    weights = args[9:]
    groups, own_lat, depth = lat.shape
    own_in = inp.shape[1]
    width = CHUNK
    rows = depth // members
    ins = mask.shape[1]
    spots = ins // own_in
    latents = own_lat * spots
    sizes = [weight.size // (rows * width) for weight in weights]
    chunks = sum(sizes)
    hidden = sizes[-1] * width
    line = members // PAIR
    heads = width // HEAD_DIM
    tiles = groups // 2 if groups % 2 == 0 else groups
    vmem = pltpu.VMEM
    vspec = pl.BlockSpec(memory_space=pltpu.VMEM)
    anywhere = pl.BlockSpec(memory_space=pl.ANY)
    narrow = vmem((groups, latents, width), bf16)
    full = vmem((groups, latents, depth), bf16)
    own = vmem((groups, own_lat, depth), f32)
    gain_shape = (8, depth)
    dma = pltpu.SemaphoreType.DMA
    wspecs = [
        vspec if turned and index in TURNED else anywhere for index in range(len(weights))
    ]
    return pl.pallas_call(
        functools.partial(block_kernel, members, turned),
        out_shape=(
            jax.ShapeDtypeStruct((groups, own_lat, depth), bf16),
            jax.ShapeDtypeStruct((groups, own_lat, depth), f32),
            jax.ShapeDtypeStruct((groups, own_in, depth), f32),
            jax.ShapeDtypeStruct(gain_shape, f32),
            jax.ShapeDtypeStruct((chunks, rows, width), f32),
        ),
        in_specs=[vspec] * 4
        + [pl.BlockSpec(memory_space=pltpu.SMEM)]
        + [vspec] * 4
        + wspecs,
        out_specs=(vspec,) * 5,
        scratch_shapes=[
            vmem((groups, 1, ins), f32),
            vmem((chunks, depth, width), bf16),
            vmem((chunks, depth, width), bf16),
            vmem((chunks, line * rows, width), bf16),
            vmem((chunks, (line - 1) * rows, width), bf16),
            vmem((groups, ins, depth), bf16),
            full,
            full,
            full,
            vmem((groups, ins, 2 * width), bf16),
            vmem((groups, ins, 2 * width), bf16),
        ]
        + [narrow] * 11
        + [
            vmem((groups, heads, latents, ins), f32),
            vmem((groups, heads, latents, latents), f32),
            vmem((groups, latents, hidden), f32),
            vmem((groups, latents, hidden), bf16),
            vmem((groups, latents, hidden), bf16),
            full,
            full,
            full,
            own,
            own,
            own,
            own,
            full,
            full,
            vmem((2, 2, groups, own_lat, depth), bf16),
            vmem((2, groups, own_lat, depth), bf16),
            vmem((groups, 2, depth // width, own_in, width), bf16),
            vmem((groups, depth // width, own_in, width), bf16),
            vmem(gain_shape, f32),
            vmem((3,) + gain_shape, f32),
            vmem((3,) + gain_shape, f32),
            vmem((line,) + gain_shape, f32),
            dma,
            dma((4, chunks)),
            dma((4, chunks)),
            dma((6 * tiles, 6)),
            dma((6 * tiles, 4)),
            dma((groups, 6)),
            dma((groups, 4)),
            dma((chunks, 2, min(line, 4) - 1)),
            dma((2, 4)),
        ],
        compiler_params=pltpu.CompilerParams(
            collective_id=0, has_side_effects=True, vmem_limit_bytes=VMEM_TOP
        ),
    )(*args)


TURNED = (3, 7, 9)


def finish_kernel(sizes, turned, *refs):
    count = len(sizes)
    ins, outs = refs[:5], refs[5 : 12 + count]
    held, parts, gain_rows, flipped, in_sems, out_sems = refs[12 + count :]
    chunks, rows, width = parts.shape
    here = held
    started = []

    def begin(source, target):
        copy = pltpu.make_async_copy(source, target, out_sems.at[len(started)])
        copy.start()
        started.append(copy)

    passing = (ins[0], ins[1], ins[2], ins[3])
    loads = [
        pltpu.make_async_copy(source, target, in_sems.at[index])
        for index, (source, target) in enumerate(zip(passing, here))
    ]
    pieces = [
        pltpu.make_async_copy(ins[4].at[chunk], parts.at[chunk], in_sems.at[4 + chunk])
        for chunk in range(chunks)
    ]
    loads[2].start()
    for piece in pieces:
        piece.start()
    for index in (1, 0, 3):
        loads[index].start()
    loads[2].wait()
    begin(here[2], outs[2])
    chunk, turn = 0, 0
    for index, size in enumerate(sizes):
        for piece in range(size):
            pieces[chunk].wait()
            out = outs[7 + index]
            at = slice(piece * width, (piece + 1) * width)
            if chunk in turned:
                flipped[turn] = parts[chunk].T
                begin(flipped.at[turn], out.at[at, :])
                turn += 1
            else:
                begin(parts.at[chunk], out.at[:, at])
            chunk += 1
    for index in (1, 0):
        loads[index].wait()
        begin(here[index], outs[index])
    loads[3].wait()
    for index in range(4):
        gain_rows[index] = here[3][index : index + 1, :]
        begin(gain_rows.at[index], outs[3 + index])
    for copy in started:
        copy.wait()


def finish(turned, sizes, block_out, grad_lat, grad_in, grad_gain, grad_w):
    chunks, rows, width = grad_w.shape
    depth = block_out.shape[-1]
    passing = (block_out, grad_lat, grad_in)
    shapes = [jax.ShapeDtypeStruct(value.shape, value.dtype) for value in passing]
    shapes += [jax.ShapeDtypeStruct((1, depth), f32)] * 4
    first = 0
    for size in sizes:
        shape = (width * size, rows) if first in turned else (rows, width * size)
        shapes.append(jax.ShapeDtypeStruct(shape, f32))
        first += size
    anywhere = pl.BlockSpec(memory_space=pl.ANY)
    vmem, dma = pltpu.VMEM, pltpu.SemaphoreType.DMA
    return pl.pallas_call(
        functools.partial(finish_kernel, sizes, turned),
        out_shape=tuple(shapes),
        in_specs=[anywhere] * 5,
        out_specs=(anywhere,) * len(shapes),
        scratch_shapes=[
            [vmem(value.shape, value.dtype) for value in passing + (grad_gain,)],
            vmem(grad_w.shape, f32),
            vmem((4, 1, depth), f32),
            vmem((max(len(turned), 1), width, rows), f32),
            dma((4 + chunks,)),
            dma((7 + chunks,)),
        ],
        compiler_params=pltpu.CompilerParams(vmem_limit_bytes=VMEM_TOP),
    )(block_out, grad_lat, grad_in, grad_gain, grad_w)


def per_device(members, *args):
    (latents, inputs, input_masks, valid_counts) = args[:4]
    gain_set, weights, out_cotangent = args[4:8], args[8:18], args[18]
    depth = latents.shape[2]
    rows = depth // members
    inside = rows % 128 == 0
    sizes = [weight.size // (rows * CHUNK) for weight in weights]
    turned, first = [], 0
    for index, size in enumerate(sizes):
        if inside and index in TURNED:
            turned += range(first, first + size)
        first += size
    turned = tuple(turned)
    if not inside:
        weights = [w.T if index in TURNED else w for index, w in enumerate(weights)]
    gains = [gain.reshape(1, depth) for gain in gain_set]
    done = run_block(
        members,
        turned,
        latents,
        inputs,
        out_cotangent,
        input_masks,
        valid_counts,
        *gains,
        *weights,
    )
    done = finish(turned, sizes, *done)
    grads = done[7:]
    if not inside:
        grads = [g.T if index in TURNED else g for index, g in enumerate(grads)]
    return (*done[:3], *[gain.reshape(depth) for gain in done[3:7]], *grads)


def solution(mesh):
    rows_first = P("dp", "head")
    cols_first = P("head", "dp")
    tokens = P("dp", "head", None)
    weight_specs = tuple(cols_first if index in TURNED else rows_first for index in range(10))
    in_specs = (tokens, tokens, P("dp", None), P("dp"), P(), P(), P(), P(), *weight_specs, tokens)
    out_specs = (tokens, tokens, tokens, P(), P(), P(), P(), *weight_specs)
    return jax.shard_map(
        functools.partial(per_device, mesh.shape["dp"]),
        mesh=mesh,
        in_specs=in_specs,
        out_specs=out_specs,
        check_vma=False,
    )
```

```python
import functools
import typing

import jax
import jax.numpy as jnp
from jax import lax
from jax.experimental import pallas as pl
from jax.experimental.pallas import tpu as pltpu
from jax.sharding import PartitionSpec as P

HEAD_DIM = 128
CHUNK = 256
PAIR = 2
CORES = 2
MESH = pl.DeviceIdType.MESH
VMEM_TOP = 64 * 1024 * 1024 - 64 * 1024

QC, KC, VC, OC, QS, KS, VS, OS, UP = 0, 1, 2, 3, 4, 5, 6, 7, 8

FOLD_SLOT = (0, 1, 0, 1, 0, 0)

bf16 = jnp.bfloat16
f32 = jnp.float32
epsilon = 1e-05


def dot(left, right):
    return lax.dot_general(left, right, (((1,), (0,)), ((), ())), preferred_element_type=f32)


def dot_t(left, right):
    return lax.dot_general(left, right, (((1,), (1,)), ((), ())), preferred_element_type=f32)


def t_dot(left, right):
    return lax.dot_general(left, right, (((0,), (0,)), ((), ())), preferred_element_type=f32)


def norm_parts(rows):
    centered = rows - jnp.mean(rows, axis=-1, keepdims=True)
    scale = lax.rsqrt(jnp.mean(centered * centered, axis=-1, keepdims=True) + epsilon)
    return centered * scale, scale


def gelu_parts(pre):
    bend = 0.7978845608028654 * (pre + 0.044715 * pre * pre * pre)
    return 0.5 * (1.0 + jnp.tanh(bend))


def gelu_slope(pre):
    squared = pre * pre
    tanh = jnp.tanh(0.7978845608028654 * (pre + 0.044715 * pre * squared))
    inner = 0.7978845608028654 * (1.0 + 3 * 0.044715 * squared)
    return 0.5 * (1.0 + tanh) + 0.5 * pre * (1.0 - tanh * tanh) * inner


def loop(count, body):
    def step(index, carry):
        body(index)
        return carry

    lax.fori_loop(0, count, step, 0)


def flat(value):
    return value.reshape(-1, value.shape[-1])


def push(source, target, send_sem, recv_sem, place):
    pltpu.make_async_remote_copy(
        src_ref=source,
        dst_ref=target,
        send_sem=send_sem,
        recv_sem=recv_sem,
        device_id=place,
        device_id_type=MESH,
    ).start()


def drain(like, sem):
    pltpu.make_async_copy(like, like, sem).wait()


class Refs(typing.NamedTuple):
    lat: typing.Any
    inp: typing.Any
    cot: typing.Any
    mask: typing.Any
    counts: typing.Any
    gain_input: typing.Any
    gain_cross: typing.Any
    gain_self: typing.Any
    gain_mlp: typing.Any
    query_cross: typing.Any
    key_cross: typing.Any
    value_cross: typing.Any
    output_cross: typing.Any
    query_self: typing.Any
    key_self: typing.Any
    value_self: typing.Any
    output_self: typing.Any
    mlp_up: typing.Any
    mlp_down: typing.Any
    block_out: typing.Any
    grad_lat: typing.Any
    grad_in: typing.Any
    grad_gain: typing.Any
    grad_w: typing.Any
    allow: typing.Any
    full_w: typing.Any
    part_w: typing.Any
    pair_buf: typing.Any
    line_buf: typing.Any
    normed_in: typing.Any
    normed_lat: typing.Any
    normed_two: typing.Any
    normed_three: typing.Any
    keys: typing.Any
    grad_keys: typing.Any
    q_one: typing.Any
    o_one: typing.Any
    q_two: typing.Any
    k_two: typing.Any
    v_two: typing.Any
    o_two: typing.Any
    gq_one: typing.Any
    gq_two: typing.Any
    gk_two: typing.Any
    gv_two: typing.Any
    grad_att: typing.Any
    prob_one: typing.Any
    prob_two: typing.Any
    pre: typing.Any
    act: typing.Any
    grad_pre: typing.Any
    spread_out: typing.Any
    spread_two: typing.Any
    spread_one: typing.Any
    hidden_one: typing.Any
    hidden_two: typing.Any
    grad_two: typing.Any
    grad_one: typing.Any
    partial: typing.Any
    partial_out: typing.Any
    fold_core: typing.Any
    fold_row: typing.Any
    in_core: typing.Any
    in_row: typing.Any
    gain_mine: typing.Any
    gain_head: typing.Any
    gain_sum: typing.Any
    gain_recv: typing.Any
    gain_line: typing.Any
    own_sem: typing.Any
    gather_sems: typing.Any
    scatter_sems: typing.Any
    spread_sems: typing.Any
    fold_sems: typing.Any
    in_sems: typing.Any
    in_fold_sems: typing.Any
    relay_sems: typing.Any
    gain_sems: typing.Any


def block_kernel(members, turned, *refs):
    r = Refs(*refs)
    groups, own_lat, depth = r.lat.shape
    own_in = r.inp.shape[1]
    hidden = r.act.shape[2]
    chunks, rows, width = r.grad_w.shape
    heads = width // HEAD_DIM
    downs = hidden // width
    down = UP + downs
    scaling = HEAD_DIM ** (-0.5)
    pairs = 2 if groups % 2 == 0 else 1
    tiles = groups // pairs

    me = lax.axis_index("dp")
    line = members // PAIR
    row, column = me // PAIR, me % PAIR
    partner = {"dp": row * PAIR + 1 - column}
    spot = lax.axis_index("head")
    side, core = spot // CORES, spot % CORES
    spot_core = side * CORES + 1 - core
    spot_row = (1 - side) * CORES + core
    spot_both = (1 - side) * CORES + 1 - core
    to_core = {"head": spot_core}
    to_row = {"head": spot_row}
    to_both = {"head": spot_both}

    def line_peer(step):
        return lax.rem(row + step, line)

    def member(other):
        return {"dp": other * PAIR + column}

    barrier = pltpu.get_barrier_semaphore()
    for place in (partner, to_core, to_row, to_both):
        pl.semaphore_signal(barrier, inc=1, device_id=place, device_id_type=MESH)

    def hello(step, carry):
        pl.semaphore_signal(
            barrier, inc=1, device_id=member(line_peer(step)), device_id_type=MESH
        )
        return carry

    lax.fori_loop(1, line, hello, 0)
    pl.semaphore_wait(barrier, line + 3)

    full_w, part_w = r.full_w, r.part_w
    gather_sems, scatter_sems = r.gather_sems, r.scatter_sems

    downs_from = chunks - (chunks - UP) // 2

    def holder(chunk):
        if chunk >= downs_from:
            return r.mlp_down, chunk - downs_from
        if chunk >= UP:
            return r.mlp_up, chunk - UP
        whole = (
            r.query_cross,
            r.key_cross,
            r.value_cross,
            r.output_cross,
            r.query_self,
            r.key_self,
            r.value_self,
            r.output_self,
        )
        return whole[chunk], 0

    def shard(chunk):
        weight, piece = holder(chunk)
        if chunk in turned:
            return block(chunk, me)
        return weight.at[:, piece * width : (piece + 1) * width]

    def block(chunk, other):
        return full_w.at[chunk, pl.ds(pl.multiple_of(other * rows, rows), rows), :]

    hops = line - 1 if line <= 4 else 1
    relayed = line <= 4
    twice = (7, 13) if relayed else ()
    relay_sems = r.relay_sems
    ticks = [0]

    def span(chunk, other):
        if chunk in twice:
            first = pl.multiple_of(other * PAIR * rows, PAIR * rows)
            return full_w.at[chunk, pl.ds(first, PAIR * rows), :]
        return block(chunk, other * PAIR + column)

    def gather_direct(chunk):
        def one(step, carry):
            push(
                shard(chunk),
                block(chunk, me),
                gather_sems.at[0, chunk],
                gather_sems.at[1, chunk],
                member(line_peer(step)),
            )
            return carry

        lax.fori_loop(1, line, one, 0)

    def gather_pair(chunk):
        push(
            shard(chunk),
            block(chunk, me),
            gather_sems.at[2, chunk],
            gather_sems.at[3, chunk],
            partner,
        )

    def along(chunk, source, target, way, hop):
        @pl.when((row + way >= 0) & (row + way < line))
        def _():
            push(
                source,
                target,
                gather_sems.at[0, chunk],
                relay_sems.at[chunk, (1 - way) // 2, hop],
                member(row + way),
            )

    def gather_start(chunk):
        if not relayed:
            gather_direct(chunk)
            return
        source, target = shard(chunk), block(chunk, me)
        if chunk in twice:
            drain(target, gather_sems.at[3, chunk])
            source = target = span(chunk, row)
        for way in (1, -1):
            along(chunk, source, target, way, 0)

    def relay(chunk, hop):
        for way in (1, -1):
            other = row - way * hop

            @pl.when((other >= 0) & (other < line))
            def _():
                got = span(chunk, other)
                drain(got, relay_sems.at[chunk, (1 - way) // 2, hop - 1])
                if hop < line - 1:
                    along(chunk, got, got, way, hop)
                if chunk not in twice:
                    push(got, got, gather_sems.at[2, chunk], gather_sems.at[3, chunk], partner)

    def forward_direct(chunk):
        drain(full_w.at[chunk, pl.ds(0, (line - 1) * rows), :], gather_sems.at[1, chunk])

        def one(step, carry):
            source = block(chunk, line_peer(step) * PAIR + column)
            push(source, source, gather_sems.at[2, chunk], gather_sems.at[3, chunk], partner)
            return carry

        lax.fori_loop(1, line, one, 0)

    def tick():
        now = ticks[0]
        ticks[0] = now + 1
        for hop in range(1, hops + 1):
            if 0 <= now - hop + 1 < chunks:
                (relay if relayed else lambda chunk, _: forward_direct(chunk))(now - hop + 1, hop)
        if now + 3 < chunks:
            gather_start(now + 3)
        if now + ahead < chunks and now + ahead not in twice:
            gather_pair(now + ahead)

    def ticked(count):
        while ticks[0] < min(count, chunks + hops - 1):
            tick()

    def have_weights(chunk):
        ticked(chunk + hops)
        if chunk not in twice:
            drain(full_w.at[chunk, pl.ds(0, line * rows), :], gather_sems.at[3, chunk])

    def gather_sent(chunk):
        size = PAIR if chunk in twice else 1
        count = line - 1
        if relayed:
            count = jnp.where(row < line - 1, row + 1, 0) + jnp.where(row > 0, line - row, 0)
        like = full_w.at[chunk, pl.ds(0, size * rows), :]
        loop(count, lambda index: drain(like, gather_sems.at[0, chunk]))
        back = 1 if chunk in twice else line
        drain(full_w.at[chunk, pl.ds(0, back * rows), :], gather_sems.at[2, chunk])

    ahead = min(3, chunks)

    def part(index):
        return pl.ds(pl.multiple_of(index * rows, rows), rows)

    pair_buf, line_buf, total = r.pair_buf, r.line_buf, r.grad_w

    line_first = tuple(range(downs_from, downs_from + 1)) if line == 4 else ()

    def both(other):
        return pl.ds(pl.multiple_of(other * PAIR * rows, PAIR * rows), PAIR * rows)

    def arrival(chunk, step):
        if step < line - 1:
            return pair_buf.at[chunk, pl.ds((step - 1) * PAIR * rows, PAIR * rows), :]
        return line_buf.at[chunk, pl.ds(0, PAIR * rows), :]

    def line_like(chunk):
        return part_w.at[chunk, pl.ds(0, (line - 1) * PAIR * rows), :]

    def first_line(chunk):
        for step in (2, 1, 3):
            other = line_peer(step)
            push(
                part_w.at[chunk, both(other), :],
                arrival(chunk, step),
                scatter_sems.at[2, chunk],
                scatter_sems.at[3, chunk],
                member(other),
            )

    def then_pair(chunk):
        drain(line_like(chunk), scatter_sems.at[3, chunk])
        for where in (1 - column, column):
            first = pl.ds(pl.multiple_of(where * rows, rows), rows)
            value = part_w[chunk, part(row * PAIR + where), :].astype(f32)
            for step in range(1, line):
                value = value + arrival(chunk, step)[first, :].astype(f32)
            if where is column:
                total[chunk] = value
                continue
            part_w[chunk, part(row * PAIR + where), :] = value.astype(bf16)
            push(
                part_w.at[chunk, part(row * PAIR + where), :],
                line_buf.at[chunk, pl.ds(PAIR * rows, rows), :],
                scatter_sems.at[0, chunk],
                scatter_sems.at[1, chunk],
                partner,
            )

    def scatter_pair(chunk):
        if chunk in line_first:
            first_line(chunk)
            return
        def one(other):
            push(
                part_w.at[chunk, part(other * PAIR + 1 - column), :],
                pair_buf.at[chunk, part(other), :],
                scatter_sems.at[0, chunk],
                scatter_sems.at[1, chunk],
                partner,
            )

        loop(line, one)

    def scatter_line(chunk):
        if chunk in line_first:
            then_pair(chunk)
            return
        drain(pair_buf.at[chunk], scatter_sems.at[1, chunk])
        own = part_w[chunk, part(me), :].astype(f32)
        total[chunk] = own + pair_buf[chunk, part(row), :].astype(f32)

        def one(step, carry):
            other = line_peer(step)
            mine = part_w[chunk, part(other * PAIR + column), :].astype(f32)
            theirs = pair_buf[chunk, part(other), :].astype(f32)
            pair_buf[chunk, part(other), :] = (mine + theirs).astype(bf16)
            push(
                pair_buf.at[chunk, part(other), :],
                line_buf.at[chunk, part(step - 1), :],
                scatter_sems.at[2, chunk],
                scatter_sems.at[3, chunk],
                member(other),
            )
            return carry

        lax.fori_loop(1, line, one, 0)

    order = []
    lined = [0]

    def send_pair(chunk):
        order.append(chunk)
        scatter_pair(chunk)

    def line_ticked(count):
        while lined[0] < min(count, len(order)):
            scatter_line(order[lined[0]])
            lined[0] += 1

    def scatter_end(chunk):
        if chunk in line_first:
            last = line_buf.at[chunk, pl.ds(PAIR * rows, rows), :]
            drain(last, scatter_sems.at[1, chunk])
            total[chunk] += last[...].astype(f32)
            return
        drain(line_buf.at[chunk], scatter_sems.at[3, chunk])

        def one(step, carry):
            total[chunk] += line_buf[chunk, part(step - 1), :].astype(f32)
            return carry

        lax.fori_loop(1, line, one, 0)

    spread_sems, fold_sems = r.spread_sems, r.fold_sems

    def mine(spot_at):
        return pl.ds(pl.multiple_of(spot_at * own_lat, own_lat), own_lat)

    def mine_in(spot_at):
        return pl.ds(pl.multiple_of(spot_at * own_in, own_in), own_in)

    def some(half):
        return pl.ds(half * pairs, pairs)

    def slot(use, half):
        return use * tiles + half

    def spread_first(full, use, half):
        own = full.at[some(half), mine(spot), :]
        at = slot(use, half)
        push(own, own, spread_sems.at[at, 0], spread_sems.at[at, 1], to_row)
        push(own, own, spread_sems.at[at, 2], spread_sems.at[at, 3], to_core)

    def spread_next(full, use, half):
        got = full.at[some(half), mine(spot_row), :]
        at = slot(use, half)
        drain(got, spread_sems.at[at, 1])
        push(got, got, spread_sems.at[at, 4], spread_sems.at[at, 5], to_core)

    def spread_last(full, use, half):
        like = full.at[some(half), mine(spot), :]
        drain(like, spread_sems.at[slot(use, half), 3])
        drain(like, spread_sems.at[slot(use, half), 5])

    def spread_sent(full, use, half):
        for which in (0, 2, 4):
            drain(full.at[some(half), mine(spot), :], spread_sems.at[slot(use, half), which])

    fold_core, fold_row = r.fold_core, r.fold_row

    def fold_first(whole, use, half):
        for place, spot_at in enumerate((spot_core, spot_both)):
            push(
                whole.at[some(half), mine(spot_at), :],
                fold_core.at[FOLD_SLOT[use], place, some(half)],
                fold_sems.at[slot(use, half), 0],
                fold_sems.at[slot(use, half), 1],
                to_core,
            )

    def fold_next(whole, use, half):
        drain(fold_core.at[FOLD_SLOT[use], :, some(half)], fold_sems.at[slot(use, half), 1])
        for group in range(half * pairs, half * pairs + pairs):
            near = whole[group, mine(spot_row), :].astype(f32)
            far = fold_core[FOLD_SLOT[use], 1, group].astype(f32)
            whole[group, mine(spot_row), :] = (near + far).astype(bf16)
        push(
            whole.at[some(half), mine(spot_row), :],
            fold_row.at[FOLD_SLOT[use], some(half)],
            fold_sems.at[slot(use, half), 2],
            fold_sems.at[slot(use, half), 3],
            to_row,
        )

    def fold_last(use, half):
        drain(fold_row.at[FOLD_SLOT[use], some(half)], fold_sems.at[slot(use, half), 3])

    def folded(whole, use, group):
        near = whole[group, mine(spot), :].astype(f32) + fold_core[FOLD_SLOT[use], 0, group].astype(f32)
        return near + fold_row[FOLD_SLOT[use], group].astype(f32)

    def fold_sent(use, half):
        drain(fold_core.at[FOLD_SLOT[use], :, some(half)], fold_sems.at[slot(use, half), 0])
        drain(fold_row.at[FOLD_SLOT[use], some(half)], fold_sems.at[slot(use, half), 2])

    in_sems, in_fold_sems = r.in_sems, r.in_fold_sems
    normed_in = r.normed_in

    def in_first(group):
        own = normed_in.at[group, mine_in(spot), :]
        push(own, own, in_sems.at[group, 0], in_sems.at[group, 1], to_row)
        push(own, own, in_sems.at[group, 2], in_sems.at[group, 3], to_core)

    def in_next(group):
        got = normed_in.at[group, mine_in(spot_row), :]
        drain(got, in_sems.at[group, 1])
        push(got, got, in_sems.at[group, 4], in_sems.at[group, 5], to_core)

    def in_last(group):
        like = normed_in.at[group, mine_in(spot), :]
        drain(like, in_sems.at[group, 3])
        drain(like, in_sems.at[group, 5])

    def in_sent(group):
        for which in (0, 2, 4):
            drain(normed_in.at[group, mine_in(spot), :], in_sems.at[group, which])

    in_core, in_row = r.in_core, r.in_row
    ins = normed_in.shape[1]
    blocks, stacked = depth // width, depth // ins

    def dn_in(group, piece, at):
        first = piece % stacked * ins
        if not isinstance(piece, int):
            first = pl.multiple_of(first, ins)
        index = UP + (group * blocks + piece) // stacked
        return full_w.at[index, pl.ds(first + at.start, at.size), :]

    def in_fold_first(group):
        for place, spot_at in enumerate((spot_core, spot_both)):
            for piece in range(blocks):
                push(
                    dn_in(group, piece, mine_in(spot_at)),
                    in_core.at[group, place, piece],
                    in_fold_sems.at[group, 0],
                    in_fold_sems.at[group, 1],
                    to_core,
                )

    def in_fold_next(group):
        drain(in_core.at[group], in_fold_sems.at[group, 1])
        for piece in range(blocks):
            own = dn_in(group, piece, mine_in(spot_row))
            own[...] = (own[...].astype(f32) + in_core[group, 1, piece].astype(f32)).astype(bf16)
            push(
                own,
                in_row.at[group, piece],
                in_fold_sems.at[group, 2],
                in_fold_sems.at[group, 3],
                to_row,
            )

    lat, inp, cot = r.lat, r.inp, r.cot
    all_gains = (r.gain_input, r.gain_cross, r.gain_self, r.gain_mlp)

    def gain(index):
        return all_gains[index][...]

    def lanes(index, size=width):
        return pl.ds(pl.multiple_of(index * size, size), size)

    def project(target, source, chunk, half):
        value = dot(flat(source[some(half)]), full_w[chunk])
        target[some(half)] = value.astype(bf16).reshape(pairs, -1, width)

    def project_back(target, terms, half):
        def one(piece):
            value = None
            for source, first, chunk in terms:
                term = dot_t(
                    flat(source[some(half), :, first : first + width]),
                    full_w[chunk, lanes(piece), :],
                )
                value = term if value is None else value + term
            target[some(half), :, lanes(piece)] = value.astype(bf16).reshape(pairs, -1, width)

        loop(blocks, one)

    def weight_grad(chunk, left, right, first=0, send=True):
        def one(index):
            value = None
            for group in range(0, groups, pairs):
                for_rows = pl.ds(group, pairs)
                term = t_dot(
                    flat(left[for_rows, :, lanes(index)]),
                    flat(right[for_rows, :, first : first + width]),
                )
                value = term if value is None else value + term
            part_w[chunk, lanes(index), :] = value.astype(bf16)

        loop(blocks, one)
        if send:
            send_pair(chunk)

    def each(half, body):
        loop(pairs, lambda index: body(half * pairs + index))

    def attend(group, queries, keys, key_at, values, value_at, prob, target, masked):
        for head in range(heads):
            at = head * HEAD_DIM
            query = queries[group, :, at : at + HEAD_DIM]
            key = keys[group, :, key_at + at : key_at + at + HEAD_DIM]
            value = values[group, :, value_at + at : value_at + at + HEAD_DIM]
            scores = dot_t(query, key) * scaling
            if masked:
                scores = jnp.where(r.allow[group] > 0.5, scores, -1e30)
            grown = jnp.exp(scores - jnp.max(scores, axis=-1, keepdims=True))
            share = grown / jnp.sum(grown, axis=-1, keepdims=True)
            prob[group, head] = share
            target[group, :, at : at + HEAD_DIM] = dot(share.astype(bf16), value).astype(bf16)

    def attend_back(group, queries, keys, key_at, values, value_at, prob, grad, outs):
        (gq, gk, gk_at, gv, gv_at) = outs
        for head in range(heads):
            at = head * HEAD_DIM
            query = queries[group, :, at : at + HEAD_DIM]
            key = keys[group, :, key_at + at : key_at + at + HEAD_DIM]
            value = values[group, :, value_at + at : value_at + at + HEAD_DIM]
            back = grad[group, :, at : at + HEAD_DIM]
            share = prob[group, head]
            slope = dot_t(back, value)
            slope = share * (slope - jnp.sum(share * slope, axis=-1, keepdims=True))
            slope = slope.astype(bf16)
            gq[group, :, at : at + HEAD_DIM] = (dot(slope, key) * scaling).astype(bf16)
            gk[group, :, gk_at + at : gk_at + at + HEAD_DIM] = (
                t_dot(slope, query) * scaling
            ).astype(bf16)
            gv[group, :, gv_at + at : gv_at + at + HEAD_DIM] = t_dot(
                share.astype(bf16), back
            ).astype(bf16)

    gain_mine = r.gain_mine
    gain_mine[...] = jnp.zeros_like(gain_mine)

    def norm_back(rows_in, index, grad):
        shaped, scale = norm_parts(rows_in)
        gain_mine[index : index + 1, :] += jnp.sum(grad * shaped, axis=0, keepdims=True)
        grad = grad * gain(index)
        center = jnp.mean(grad, axis=-1, keepdims=True)
        along = jnp.mean(grad * shaped, axis=-1, keepdims=True)
        return (grad - center - shaped * along) * scale

    GAIN_INPUT, GAIN_CROSS, GAIN_SELF, GAIN_MLP = 0, 1, 2, 3

    straight = [chunk for chunk in range(chunks) if chunk not in turned]
    for chunk in turned:
        weight, piece = holder(chunk)
        value = weight[piece * width : (piece + 1) * width, :].astype(f32)
        full_w[chunk, pl.ds(pl.multiple_of(me * rows, rows), rows), :] = value.T.astype(bf16)
    for chunk in straight:
        pltpu.make_async_copy(shard(chunk), block(chunk, me), r.own_sem).start()
    for chunk in range(chunks):
        if chunk < ahead or chunk in twice:
            gather_pair(chunk)
    for chunk in range(min(3, chunks)):
        gather_start(chunk)
    halves = range(tiles)

    def lat_rows(group):
        shaped, _ = norm_parts(lat[group].astype(f32))
        r.normed_lat[group, mine(spot), :] = (shaped * gain(GAIN_CROSS)).astype(bf16)

    for half in halves:
        each(half, lat_rows)
        spread_first(r.normed_lat, 0, half)

    def in_rows(group):
        shaped, _ = norm_parts(inp[group].astype(f32))
        normed_in[group, mine_in(spot), :] = (shaped * gain(GAIN_INPUT)).astype(bf16)
        in_first(group)

    for group in range(groups):
        in_rows(group)
        if group < 3:
            ticked(group + 1)
    r.spread_out[:, mine(spot), :] = cot[...]
    for half in halves:
        spread_first(r.spread_out, 3, half)
    for half in halves:
        spread_next(r.normed_lat, 0, half)
    in_next(0)
    drain(full_w.at[pl.ds(0, len(straight)), pl.ds(0, rows), :], r.own_sem)
    positions = lax.broadcasted_iota(jnp.int32, (1, ins), 1)
    for group in range(groups):
        allowed = (positions < r.counts[group]) & (
            (r.mask[group : group + 1, :] == 1) | (positions == 0)
        )
        r.allow[group] = allowed.astype(f32)
    ticked(4)
    have_weights(QC)
    for half in halves:
        spread_last(r.normed_lat, 0, half)
        project(r.q_one, r.normed_lat, QC, half)
    if groups > 1:
        in_next(1)
    have_weights(KC)
    have_weights(VC)
    keys = r.keys
    piece_rows = min(256, ins)

    def key_rows(group):
        in_last(group)
        for piece in range(ins // piece_rows):
            at = slice(piece * piece_rows, piece * piece_rows + piece_rows)
            keys[group, at, :width] = dot(normed_in[group, at, :], full_w[KC]).astype(bf16)
            keys[group, at, width:] = dot(normed_in[group, at, :], full_w[VC]).astype(bf16)
        attend(group, r.q_one, keys, 0, keys, width, r.prob_one, r.o_one, True)

    for group in range(groups):
        key_rows(group)
        ticked(6 + group)
        if 2 + group < groups:
            in_next(2 + group)
        half = group // pairs
        if group % pairs == pairs - 1:
            if half == 0:
                have_weights(OC)
            project_back(r.partial, [(r.o_one, 0, OC)], half)
            fold_first(r.partial, 0, half)
        elif half > 0:
            fold_next(r.partial, 0, half - 1)
    for half in halves:
        spread_next(r.spread_out, 3, half)
    for half in range(tiles - 1 if pairs > 1 else 0, tiles):
        fold_next(r.partial, 0, half)

    def one_rows(group):
        rows_now = lat[group].astype(f32) + folded(r.partial, 0, group)
        r.hidden_one[group] = rows_now
        shaped, _ = norm_parts(rows_now)
        r.normed_two[group, mine(spot), :] = (shaped * gain(GAIN_SELF)).astype(bf16)

    for half in halves:
        fold_last(0, half)
        each(half, one_rows)
        spread_first(r.normed_two, 1, half)
        ticked(10 + half)
    for half in halves:
        spread_next(r.normed_two, 1, half)
    have_weights(QS)
    have_weights(KS)
    have_weights(VS)

    def self_rows(group):
        attend(group, r.q_two, r.k_two, 0, r.v_two, 0, r.prob_two, r.o_two, False)

    for half in halves:
        spread_last(r.normed_two, 1, half)
        for target, chunk in ((r.q_two, QS), (r.k_two, KS), (r.v_two, VS)):
            project(target, r.normed_two, chunk, half)
        each(half, self_rows)
        if half == 0:
            have_weights(OS)
        ticked(12 + half)
        fold_sent(0, half)
        project_back(r.partial, [(r.o_two, 0, OS)], half)
        fold_first(r.partial, 1, half)
        if half > 0:
            fold_next(r.partial, 1, half - 1)
    fold_next(r.partial, 1, tiles - 1)
    ticked(14)

    def two_rows(group):
        rows_now = r.hidden_one[group] + folded(r.partial, 1, group)
        r.hidden_two[group] = rows_now
        shaped, _ = norm_parts(rows_now)
        r.normed_three[group, mine(spot), :] = (shaped * gain(GAIN_MLP)).astype(bf16)

    for half in halves:
        fold_last(1, half)
        each(half, two_rows)
        spread_first(r.normed_three, 2, half)
        ticked(15 + half)
    for half in halves:
        spread_next(r.normed_three, 2, half)

    def up_rows(half, at):
        pre = dot(flat(r.normed_three[some(half)]), full_w[UP + at])
        r.pre[some(half), :, at * width : (at + 1) * width] = pre.reshape(pairs, -1, width)
        r.act[some(half), :, at * width : (at + 1) * width] = (
            (pre * gelu_parts(pre)).astype(bf16).reshape(pairs, -1, width)
        )

    for half in halves:
        spread_last(r.normed_three, 2, half)
        spread_last(r.spread_out, 3, half)
    for at in range(downs):
        have_weights(UP + at)
        for half in halves:
            up_rows(half, at)
        ticked(UP + downs + 4 + at)
        weight_grad(down + at, r.spread_out, r.act, at * width, send=False)

    def down_rows(half, at):
        back = dot(flat(r.spread_out[some(half)]), full_w[down + at])
        pre = flat(r.pre[some(half), :, at * width : (at + 1) * width])
        r.grad_pre[some(half), :, at * width : (at + 1) * width] = (
            (back * gelu_slope(pre)).astype(bf16).reshape(pairs, -1, width)
        )

    for at in range(downs):
        if at == downs - 1:
            ticked(chunks + hops)
            for other in range(downs):
                send_pair(down + other)
            order.insert(1, order.pop(0))
        have_weights(down + at)
        for half in halves:
            down_rows(half, at)
        if at < downs - 1:
            weight_grad(UP + at, r.normed_three, r.grad_pre, at * width, send=False)
    for half in halves:
        fold_sent(1, half)
        project_back(
            r.partial, [(r.grad_pre, at * width, UP + at) for at in range(downs)], half
        )
        fold_first(r.partial, 2, half)
    line_ticked(1)
    for at in range(downs - 1):
        send_pair(UP + at)
    weight_grad(UP + downs - 1, r.normed_three, r.grad_pre, (downs - 1) * width)
    for half in halves:
        fold_next(r.partial, 2, half)
    for half in halves:
        project_back(
            r.partial_out, [(r.act, at * width, down + at) for at in range(downs)], half
        )
        fold_first(r.partial_out, 3, half)
    line_ticked(2)

    def back_two(group):
        grad = folded(r.partial, 2, group)
        value = cot[group].astype(f32) + norm_back(r.hidden_two[group], GAIN_MLP, grad)
        r.grad_two[group] = value
        r.spread_two[group, mine(spot), :] = value.astype(bf16)

    for half in halves:
        fold_last(2, half)
        each(half, back_two)
        spread_first(r.spread_two, 4, half)
    line_ticked(3)
    for half in halves:
        spread_next(r.spread_two, 4, half)
    for half in halves:
        fold_next(r.partial_out, 3, half)
    line_ticked(4)

    def self_back(group):
        attend_back(
            group,
            r.q_two,
            r.k_two,
            0,
            r.v_two,
            0,
            r.prob_two,
            r.grad_att,
            (r.gq_two, r.gk_two, 0, r.gv_two, 0),
        )

    for half in halves:
        spread_last(r.spread_two, 4, half)
        project(r.grad_att, r.spread_two, OS, half)
        each(half, self_back)
        fold_sent(2, half)
        project_back(
            r.partial, [(r.gq_two, 0, QS), (r.gk_two, 0, KS), (r.gv_two, 0, VS)], half
        )
        fold_first(r.partial, 4, half)
        if half > 0:
            fold_next(r.partial, 4, half - 1)
        line_ticked(5 + half)
    weight_grad(OS, r.spread_two, r.o_two)
    fold_next(r.partial, 4, tiles - 1)
    weight_grad(QS, r.normed_two, r.gq_two)
    line_ticked(7)
    weight_grad(KS, r.normed_two, r.gk_two)

    def back_one(group):
        grad = folded(r.partial, 4, group)
        value = r.grad_two[group] + norm_back(r.hidden_one[group], GAIN_SELF, grad)
        r.grad_one[group] = value
        r.spread_one[group, mine(spot), :] = value.astype(bf16)

    for half in halves:
        fold_last(4, half)
        each(half, back_one)
        spread_first(r.spread_one, 5, half)
    line_ticked(8)
    weight_grad(VS, r.normed_two, r.gv_two)
    for half in halves:
        spread_next(r.spread_one, 5, half)
    line_ticked(9)

    def out_rows(group):
        r.block_out[group] = (
            r.hidden_two[group] + folded(r.partial_out, 3, group)
        ).astype(bf16)

    for chunk in range(chunks):
        gather_sent(chunk)

    def cross_back(group):
        attend_back(
            group,
            r.q_one,
            keys,
            0,
            keys,
            width,
            r.prob_one,
            r.grad_att,
            (r.gq_one, r.grad_keys, 0, r.grad_keys, width),
        )

    def in_back(group):
        for at in range(0, ins, piece_rows):

            def one(piece):
                value = dot_t(
                    r.grad_keys[group, at : at + piece_rows, :width], full_w[KC, lanes(piece), :]
                ) + dot_t(
                    r.grad_keys[group, at : at + piece_rows, width:], full_w[VC, lanes(piece), :]
                )
                dn_in(group, piece, pl.ds(at, piece_rows))[...] = value.astype(bf16)

            loop(blocks, one)
        in_fold_first(group)

    for half in halves:
        spread_last(r.spread_one, 5, half)
        if half == tiles - 1:
            weight_grad(OC, r.spread_one, r.o_one)
        project(r.grad_att, r.spread_one, OC, half)
        each(half, cross_back)
        each(half, in_back)
        line_ticked(10 + half)
    for half in halves[:1]:
        each(half, in_fold_next)
    line_ticked(12)
    weight_grad(KC, normed_in, r.grad_keys, 0)
    for half in halves[1:]:
        each(half, in_fold_next)
    weight_grad(VC, normed_in, r.grad_keys, width)
    line_ticked(13)
    for half in halves:
        fold_sent(4, half)
        project_back(r.partial, [(r.gq_one, 0, QC)], half)
        fold_first(r.partial, 5, half)
    weight_grad(QC, r.normed_lat, r.gq_one)
    for half in halves:
        fold_next(r.partial, 5, half)
    line_ticked(14)
    for half in halves:
        fold_last(3, half)
        each(half, out_rows)
    for group in range(groups):
        in_sent(group)

    def in_final(group):
        drain(in_row.at[group], in_fold_sems.at[group, 3])
        parts = []
        for piece in range(blocks):
            near = dn_in(group, piece, mine_in(spot))[...].astype(f32)
            near = near + in_core[group, 0, piece].astype(f32)
            parts.append(near + in_row[group, piece].astype(f32))
        grad = jnp.concatenate(parts, axis=-1)
        r.grad_in[group] = norm_back(inp[group].astype(f32), GAIN_INPUT, grad)

    line_ticked(15)
    each(0, in_final)
    line_ticked(16)
    for half in halves[1:]:
        each(half, in_final)

    def lat_back(group):
        grad = folded(r.partial, 5, group)
        r.grad_lat[group] = r.grad_one[group] + norm_back(
            lat[group].astype(f32), GAIN_CROSS, grad
        )

    for half in halves:
        fold_last(5, half)
        each(half, lat_back)
    gain_sems, gain_head = r.gain_sems, r.gain_head
    gain_sum, gain_recv, gain_line = r.gain_sum, r.gain_recv, r.gain_line
    spots = r.normed_in.shape[1] // own_in
    gain_head[spot] = gain_mine[...]
    for place in (to_row, to_both, to_core):
        own = gain_head.at[spot]
        push(own, own, gain_sems.at[0, 0], gain_sems.at[1, 0], place)
    drain(gain_head.at[pl.ds(0, spots - 1)], gain_sems.at[1, 0])
    whole = gain_head[0]
    for other in range(1, spots):
        whole = whole + gain_head[other]
    gain_sum[...] = whole
    push(gain_sum, gain_recv, gain_sems.at[0, 1], gain_sems.at[1, 1], partner)
    drain(gain_recv, gain_sems.at[1, 1])
    gain_line[row] = gain_sum[...] + gain_recv[...]

    def gain_send(step, carry):
        push(
            gain_line.at[row],
            gain_line.at[row],
            gain_sems.at[0, 3],
            gain_sems.at[1, 3],
            member(line_peer(step)),
        )
        return carry

    lax.fori_loop(1, line, gain_send, 0)
    for chunk in order:
        scatter_end(chunk)
    drain(gain_line.at[pl.ds(0, line - 1)], gain_sems.at[1, 3])
    whole = gain_line[0]
    for other in range(1, line):
        whole = whole + gain_line[other]
    r.grad_gain[...] = whole

    for chunk in order:
        if chunk in line_first:
            drain(line_buf.at[chunk, pl.ds(0, rows), :], scatter_sems.at[0, chunk])
            drain(line_like(chunk), scatter_sems.at[2, chunk])
        else:
            drain(pair_buf.at[chunk], scatter_sems.at[0, chunk])
            drain(line_buf.at[chunk], scatter_sems.at[2, chunk])
    spreads = (
        r.normed_lat,
        r.normed_two,
        r.normed_three,
        r.spread_out,
        r.spread_two,
        r.spread_one,
    )
    for use, full in enumerate(spreads):
        for half in halves:
            spread_sent(full, use, half)
    for half in halves:
        fold_sent(3, half)
        fold_sent(5, half)

    def in_folds_sent(group):
        drain(in_core.at[group], in_fold_sems.at[group, 0])
        drain(in_row.at[group], in_fold_sems.at[group, 2])

    loop(groups, in_folds_sent)
    drain(gain_head.at[pl.ds(0, spots - 1)], gain_sems.at[0, 0])
    drain(gain_recv, gain_sems.at[0, 1])
    drain(gain_line.at[pl.ds(0, line - 1)], gain_sems.at[0, 3])


def run_block(members, turned, *args):
    lat, inp, cot, mask = args[:4]
    weights = args[9:]
    groups, own_lat, depth = lat.shape
    own_in = inp.shape[1]
    width = CHUNK
    rows = depth // members
    ins = mask.shape[1]
    spots = ins // own_in
    latents = own_lat * spots
    sizes = [weight.size // (rows * width) for weight in weights]
    chunks = sum(sizes)
    hidden = sizes[-1] * width
    line = members // PAIR
    heads = width // HEAD_DIM
    tiles = groups // 2 if groups % 2 == 0 else groups
    vmem = pltpu.VMEM
    vspec = pl.BlockSpec(memory_space=pltpu.VMEM)
    anywhere = pl.BlockSpec(memory_space=pl.ANY)
    narrow = vmem((groups, latents, width), bf16)
    full = vmem((groups, latents, depth), bf16)
    own = vmem((groups, own_lat, depth), f32)
    gain_shape = (8, depth)
    dma = pltpu.SemaphoreType.DMA
    wspecs = [
        vspec if turned and index in TURNED else anywhere for index in range(len(weights))
    ]
    return pl.pallas_call(
        functools.partial(block_kernel, members, turned),
        out_shape=(
            jax.ShapeDtypeStruct((groups, own_lat, depth), bf16),
            jax.ShapeDtypeStruct((groups, own_lat, depth), f32),
            jax.ShapeDtypeStruct((groups, own_in, depth), f32),
            jax.ShapeDtypeStruct(gain_shape, f32),
            jax.ShapeDtypeStruct((chunks, rows, width), f32),
        ),
        in_specs=[vspec] * 4
        + [pl.BlockSpec(memory_space=pltpu.SMEM)]
        + [vspec] * 4
        + wspecs,
        out_specs=(vspec,) * 5,
        scratch_shapes=[
            vmem((groups, 1, ins), f32),
            vmem((chunks, depth, width), bf16),
            vmem((chunks, depth, width), bf16),
            vmem((chunks, line * rows, width), bf16),
            vmem((chunks, (line - 1) * rows, width), bf16),
            vmem((groups, ins, depth), bf16),
            full,
            full,
            full,
            vmem((groups, ins, 2 * width), bf16),
            vmem((groups, ins, 2 * width), bf16),
        ]
        + [narrow] * 11
        + [
            vmem((groups, heads, latents, ins), f32),
            vmem((groups, heads, latents, latents), f32),
            vmem((groups, latents, hidden), f32),
            vmem((groups, latents, hidden), bf16),
            vmem((groups, latents, hidden), bf16),
            full,
            full,
            full,
            own,
            own,
            own,
            own,
            full,
            full,
            vmem((2, 2, groups, own_lat, depth), bf16),
            vmem((2, groups, own_lat, depth), bf16),
            vmem((groups, 2, depth // width, own_in, width), bf16),
            vmem((groups, depth // width, own_in, width), bf16),
            vmem(gain_shape, f32),
            vmem((spots,) + gain_shape, f32),
            vmem(gain_shape, f32),
            vmem(gain_shape, f32),
            vmem((line,) + gain_shape, f32),
            dma,
            dma((4, chunks)),
            dma((4, chunks)),
            dma((6 * tiles, 6)),
            dma((6 * tiles, 4)),
            dma((groups, 6)),
            dma((groups, 4)),
            dma((chunks, 2, min(line, 4) - 1)),
            dma((2, 4)),
        ],
        compiler_params=pltpu.CompilerParams(
            collective_id=0, has_side_effects=True, vmem_limit_bytes=VMEM_TOP
        ),
    )(*args)


TURNED = (3, 7, 9)


def finish_kernel(sizes, turned, *refs):
    count = len(sizes)
    ins, outs = refs[:5], refs[5 : 12 + count]
    held, parts, gain_rows, flipped, in_sems, out_sems = refs[12 + count :]
    chunks, rows, width = parts.shape
    here = held
    started = []

    def begin(source, target):
        copy = pltpu.make_async_copy(source, target, out_sems.at[len(started)])
        copy.start()
        started.append(copy)

    passing = (ins[0], ins[1], ins[2], ins[3])
    loads = [
        pltpu.make_async_copy(source, target, in_sems.at[index])
        for index, (source, target) in enumerate(zip(passing, here))
    ]
    pieces = [
        pltpu.make_async_copy(ins[4].at[chunk], parts.at[chunk], in_sems.at[4 + chunk])
        for chunk in range(chunks)
    ]
    loads[2].start()
    for piece in pieces:
        piece.start()
    for index in (1, 0, 3):
        loads[index].start()
    loads[2].wait()
    begin(here[2], outs[2])
    chunk, turn = 0, 0
    for index, size in enumerate(sizes):
        for piece in range(size):
            pieces[chunk].wait()
            out = outs[7 + index]
            at = slice(piece * width, (piece + 1) * width)
            if chunk in turned:
                flipped[turn] = parts[chunk].T
                begin(flipped.at[turn], out.at[at, :])
                turn += 1
            else:
                begin(parts.at[chunk], out.at[:, at])
            chunk += 1
    for index in (1, 0):
        loads[index].wait()
        begin(here[index], outs[index])
    loads[3].wait()
    for index in range(4):
        gain_rows[index] = here[3][index : index + 1, :]
        begin(gain_rows.at[index], outs[3 + index])
    for copy in started:
        copy.wait()


def finish(turned, sizes, block_out, grad_lat, grad_in, grad_gain, grad_w):
    chunks, rows, width = grad_w.shape
    depth = block_out.shape[-1]
    passing = (block_out, grad_lat, grad_in)
    shapes = [jax.ShapeDtypeStruct(value.shape, value.dtype) for value in passing]
    shapes += [jax.ShapeDtypeStruct((1, depth), f32)] * 4
    first = 0
    for size in sizes:
        shape = (width * size, rows) if first in turned else (rows, width * size)
        shapes.append(jax.ShapeDtypeStruct(shape, f32))
        first += size
    anywhere = pl.BlockSpec(memory_space=pl.ANY)
    vmem, dma = pltpu.VMEM, pltpu.SemaphoreType.DMA
    return pl.pallas_call(
        functools.partial(finish_kernel, sizes, turned),
        out_shape=tuple(shapes),
        in_specs=[anywhere] * 5,
        out_specs=(anywhere,) * len(shapes),
        scratch_shapes=[
            [vmem(value.shape, value.dtype) for value in passing + (grad_gain,)],
            vmem(grad_w.shape, f32),
            vmem((4, 1, depth), f32),
            vmem((max(len(turned), 1), width, rows), f32),
            dma((4 + chunks,)),
            dma((7 + chunks,)),
        ],
        compiler_params=pltpu.CompilerParams(vmem_limit_bytes=VMEM_TOP),
    )(block_out, grad_lat, grad_in, grad_gain, grad_w)


def per_device(members, *args):
    (latents, inputs, input_masks, valid_counts) = args[:4]
    gain_set, weights, out_cotangent = args[4:8], args[8:18], args[18]
    depth = latents.shape[2]
    rows = depth // members
    inside = rows % 128 == 0
    sizes = [weight.size // (rows * CHUNK) for weight in weights]
    turned, first = [], 0
    for index, size in enumerate(sizes):
        if inside and index in TURNED:
            turned += range(first, first + size)
        first += size
    turned = tuple(turned)
    if not inside:
        weights = [w.T if index in TURNED else w for index, w in enumerate(weights)]
    gains = [gain.reshape(1, depth) for gain in gain_set]
    done = run_block(
        members,
        turned,
        latents,
        inputs,
        out_cotangent,
        input_masks,
        valid_counts,
        *gains,
        *weights,
    )
    done = finish(turned, sizes, *done)
    grads = done[7:]
    if not inside:
        grads = [g.T if index in TURNED else g for index, g in enumerate(grads)]
    return (*done[:3], *[gain.reshape(depth) for gain in done[3:7]], *grads)


def solution(mesh):
    rows_first = P("dp", "head")
    cols_first = P("head", "dp")
    tokens = P("dp", "head", None)
    weight_specs = tuple(cols_first if index in TURNED else rows_first for index in range(10))
    in_specs = (tokens, tokens, P("dp", None), P("dp"), P(), P(), P(), P(), *weight_specs, tokens)
    out_specs = (tokens, tokens, tokens, P(), P(), P(), P(), *weight_specs)
    return jax.shard_map(
        functools.partial(per_device, mesh.shape["dp"]),
        mesh=mesh,
        in_specs=in_specs,
        out_specs=out_specs,
        check_vma=False,
    )
```

```python
import functools
import typing

import jax
import jax.numpy as jnp
from jax import lax
from jax.experimental import pallas as pl
from jax.experimental.pallas import tpu as pltpu
from jax.sharding import PartitionSpec as P

HEAD_DIM = 128
CHUNK = 256
PAIR = 2
CORES = 2
MESH = pl.DeviceIdType.MESH
VMEM_TOP = 64 * 1024 * 1024 - 64 * 1024

QC, KC, VC, OC, QS, KS, VS, OS, UP = 0, 1, 2, 3, 4, 5, 6, 7, 8

FOLD_SLOT = (0, 1, 0, 1, 0, 0)

bf16 = jnp.bfloat16
f32 = jnp.float32
epsilon = 1e-05


def dot(left, right):
    return lax.dot_general(left, right, (((1,), (0,)), ((), ())), preferred_element_type=f32)


def dot_t(left, right):
    return lax.dot_general(left, right, (((1,), (1,)), ((), ())), preferred_element_type=f32)


def t_dot(left, right):
    return lax.dot_general(left, right, (((0,), (0,)), ((), ())), preferred_element_type=f32)


def norm_parts(rows):
    centered = rows - jnp.mean(rows, axis=-1, keepdims=True)
    scale = lax.rsqrt(jnp.mean(centered * centered, axis=-1, keepdims=True) + epsilon)
    return centered * scale, scale


def gelu_parts(pre):
    bend = 0.7978845608028654 * (pre + 0.044715 * pre * pre * pre)
    return 0.5 * (1.0 + jnp.tanh(bend))


def gelu_slope(pre):
    squared = pre * pre
    tanh = jnp.tanh(0.7978845608028654 * (pre + 0.044715 * pre * squared))
    inner = 0.7978845608028654 * (1.0 + 3 * 0.044715 * squared)
    return 0.5 * (1.0 + tanh) + 0.5 * pre * (1.0 - tanh * tanh) * inner


def loop(count, body):
    def step(index, carry):
        body(index)
        return carry

    lax.fori_loop(0, count, step, 0)


def flat(value):
    return value.reshape(-1, value.shape[-1])


def push(source, target, send_sem, recv_sem, place):
    pltpu.make_async_remote_copy(
        src_ref=source,
        dst_ref=target,
        send_sem=send_sem,
        recv_sem=recv_sem,
        device_id=place,
        device_id_type=MESH,
    ).start()


def drain(like, sem):
    pltpu.make_async_copy(like, like, sem).wait()


class Refs(typing.NamedTuple):
    lat: typing.Any
    inp: typing.Any
    cot: typing.Any
    mask: typing.Any
    counts: typing.Any
    gain_input: typing.Any
    gain_cross: typing.Any
    gain_self: typing.Any
    gain_mlp: typing.Any
    query_cross: typing.Any
    key_cross: typing.Any
    value_cross: typing.Any
    output_cross: typing.Any
    query_self: typing.Any
    key_self: typing.Any
    value_self: typing.Any
    output_self: typing.Any
    mlp_up: typing.Any
    mlp_down: typing.Any
    out_block: typing.Any
    out_lat: typing.Any
    out_in: typing.Any
    grad_gain: typing.Any
    out_w: typing.Any
    allow: typing.Any
    block_out: typing.Any
    grad_lat: typing.Any
    grad_in: typing.Any
    grad_w: typing.Any
    out_sems: typing.Any
    full_w: typing.Any
    part_w: typing.Any
    pair_buf: typing.Any
    line_buf: typing.Any
    normed_in: typing.Any
    normed_lat: typing.Any
    normed_two: typing.Any
    normed_three: typing.Any
    keys: typing.Any
    grad_keys: typing.Any
    q_one: typing.Any
    o_one: typing.Any
    q_two: typing.Any
    k_two: typing.Any
    v_two: typing.Any
    o_two: typing.Any
    gq_one: typing.Any
    gq_two: typing.Any
    gk_two: typing.Any
    gv_two: typing.Any
    grad_att: typing.Any
    prob_one: typing.Any
    prob_two: typing.Any
    pre: typing.Any
    act: typing.Any
    grad_pre: typing.Any
    spread_out: typing.Any
    spread_two: typing.Any
    spread_one: typing.Any
    hidden_one: typing.Any
    hidden_two: typing.Any
    grad_two: typing.Any
    grad_one: typing.Any
    partial: typing.Any
    partial_out: typing.Any
    fold_core: typing.Any
    fold_row: typing.Any
    in_core: typing.Any
    in_row: typing.Any
    gain_mine: typing.Any
    gain_head: typing.Any
    gain_sum: typing.Any
    gain_recv: typing.Any
    gain_line: typing.Any
    own_sem: typing.Any
    gather_sems: typing.Any
    scatter_sems: typing.Any
    spread_sems: typing.Any
    fold_sems: typing.Any
    in_sems: typing.Any
    in_fold_sems: typing.Any
    relay_sems: typing.Any
    gain_sems: typing.Any


def block_kernel(members, turned, *refs):
    r = Refs(*refs)
    groups, own_lat, depth = r.lat.shape
    own_in = r.inp.shape[1]
    hidden = r.act.shape[2]
    chunks, rows, width = r.grad_w.shape
    heads = width // HEAD_DIM
    downs = hidden // width
    down = UP + downs
    scaling = HEAD_DIM ** (-0.5)
    pairs = 2 if groups % 2 == 0 else 1
    tiles = groups // pairs

    me = lax.axis_index("dp")
    line = members // PAIR
    row, column = me // PAIR, me % PAIR
    partner = {"dp": row * PAIR + 1 - column}
    spot = lax.axis_index("head")
    side, core = spot // CORES, spot % CORES
    spot_core = side * CORES + 1 - core
    spot_row = (1 - side) * CORES + core
    spot_both = (1 - side) * CORES + 1 - core
    to_core = {"head": spot_core}
    to_row = {"head": spot_row}
    to_both = {"head": spot_both}

    def line_peer(step):
        return lax.rem(row + step, line)

    def member(other):
        return {"dp": other * PAIR + column}

    barrier = pltpu.get_barrier_semaphore()
    for place in (partner, to_core, to_row, to_both):
        pl.semaphore_signal(barrier, inc=1, device_id=place, device_id_type=MESH)

    def hello(step, carry):
        pl.semaphore_signal(
            barrier, inc=1, device_id=member(line_peer(step)), device_id_type=MESH
        )
        return carry

    lax.fori_loop(1, line, hello, 0)
    pl.semaphore_wait(barrier, line + 3)

    full_w, part_w = r.full_w, r.part_w
    gather_sems, scatter_sems = r.gather_sems, r.scatter_sems

    downs_from = chunks - (chunks - UP) // 2

    def holder(chunk):
        if chunk >= downs_from:
            return r.mlp_down, chunk - downs_from
        if chunk >= UP:
            return r.mlp_up, chunk - UP
        whole = (
            r.query_cross,
            r.key_cross,
            r.value_cross,
            r.output_cross,
            r.query_self,
            r.key_self,
            r.value_self,
            r.output_self,
        )
        return whole[chunk], 0

    def shard(chunk):
        weight, piece = holder(chunk)
        if chunk in turned:
            return block(chunk, me)
        return weight.at[:, piece * width : (piece + 1) * width]

    def block(chunk, other):
        return full_w.at[chunk, pl.ds(pl.multiple_of(other * rows, rows), rows), :]

    hops = line - 1 if line <= 4 else 1
    relayed = line <= 4
    twice = (7, 13) if relayed else ()
    relay_sems = r.relay_sems
    ticks = [0]

    def span(chunk, other):
        if chunk in twice:
            first = pl.multiple_of(other * PAIR * rows, PAIR * rows)
            return full_w.at[chunk, pl.ds(first, PAIR * rows), :]
        return block(chunk, other * PAIR + column)

    def gather_direct(chunk):
        def one(step, carry):
            push(
                shard(chunk),
                block(chunk, me),
                gather_sems.at[0, chunk],
                gather_sems.at[1, chunk],
                member(line_peer(step)),
            )
            return carry

        lax.fori_loop(1, line, one, 0)

    def gather_pair(chunk):
        push(
            shard(chunk),
            block(chunk, me),
            gather_sems.at[2, chunk],
            gather_sems.at[3, chunk],
            partner,
        )

    def along(chunk, source, target, way, hop):
        @pl.when((row + way >= 0) & (row + way < line))
        def _():
            push(
                source,
                target,
                gather_sems.at[0, chunk],
                relay_sems.at[chunk, (1 - way) // 2, hop],
                member(row + way),
            )

    def gather_start(chunk):
        if not relayed:
            gather_direct(chunk)
            return
        source, target = shard(chunk), block(chunk, me)
        if chunk in twice:
            drain(target, gather_sems.at[3, chunk])
            source = target = span(chunk, row)
        for way in (1, -1):
            along(chunk, source, target, way, 0)

    def relay(chunk, hop):
        for way in (1, -1):
            other = row - way * hop

            @pl.when((other >= 0) & (other < line))
            def _():
                got = span(chunk, other)
                drain(got, relay_sems.at[chunk, (1 - way) // 2, hop - 1])
                if hop < line - 1:
                    along(chunk, got, got, way, hop)
                if chunk not in twice:
                    push(got, got, gather_sems.at[2, chunk], gather_sems.at[3, chunk], partner)

    def forward_direct(chunk):
        drain(full_w.at[chunk, pl.ds(0, (line - 1) * rows), :], gather_sems.at[1, chunk])

        def one(step, carry):
            source = block(chunk, line_peer(step) * PAIR + column)
            push(source, source, gather_sems.at[2, chunk], gather_sems.at[3, chunk], partner)
            return carry

        lax.fori_loop(1, line, one, 0)

    def tick():
        now = ticks[0]
        ticks[0] = now + 1
        for hop in range(1, hops + 1):
            if 0 <= now - hop + 1 < chunks:
                (relay if relayed else lambda chunk, _: forward_direct(chunk))(now - hop + 1, hop)
        if now + 4 < chunks:
            gather_start(now + 4)
        if now + ahead < chunks and now + ahead not in twice:
            gather_pair(now + ahead)

    def ticked(count):
        while ticks[0] < min(count, chunks + hops - 1):
            tick()

    def have_weights(chunk):
        ticked(chunk + hops)
        if chunk not in twice:
            drain(full_w.at[chunk, pl.ds(0, line * rows), :], gather_sems.at[3, chunk])

    def gather_sent(chunk):
        size = PAIR if chunk in twice else 1
        count = line - 1
        if relayed:
            count = jnp.where(row < line - 1, row + 1, 0) + jnp.where(row > 0, line - row, 0)
        like = full_w.at[chunk, pl.ds(0, size * rows), :]
        loop(count, lambda index: drain(like, gather_sems.at[0, chunk]))
        back = 1 if chunk in twice else line
        drain(full_w.at[chunk, pl.ds(0, back * rows), :], gather_sems.at[2, chunk])

    ahead = min(3, chunks)

    def part(index):
        return pl.ds(pl.multiple_of(index * rows, rows), rows)

    pair_buf, line_buf, total = r.pair_buf, r.line_buf, r.grad_w

    line_first = tuple(range(downs_from, downs_from + 1)) if line == 4 else ()

    def both(other):
        return pl.ds(pl.multiple_of(other * PAIR * rows, PAIR * rows), PAIR * rows)

    def arrival(chunk, step):
        if step < line - 1:
            return pair_buf.at[chunk, pl.ds((step - 1) * PAIR * rows, PAIR * rows), :]
        return line_buf.at[chunk, pl.ds(0, PAIR * rows), :]

    def line_like(chunk):
        return part_w.at[chunk, pl.ds(0, (line - 1) * PAIR * rows), :]

    def first_line(chunk):
        for step in (2, 1, 3):
            other = line_peer(step)
            push(
                part_w.at[chunk, both(other), :],
                arrival(chunk, step),
                scatter_sems.at[2, chunk],
                scatter_sems.at[3, chunk],
                member(other),
            )

    def then_pair(chunk):
        drain(line_like(chunk), scatter_sems.at[3, chunk])
        for where in (1 - column, column):
            first = pl.ds(pl.multiple_of(where * rows, rows), rows)
            value = part_w[chunk, part(row * PAIR + where), :].astype(f32)
            for step in range(1, line):
                value = value + arrival(chunk, step)[first, :].astype(f32)
            if where is column:
                total[chunk] = value
                continue
            part_w[chunk, part(row * PAIR + where), :] = value.astype(bf16)
            push(
                part_w.at[chunk, part(row * PAIR + where), :],
                line_buf.at[chunk, pl.ds(PAIR * rows, rows), :],
                scatter_sems.at[0, chunk],
                scatter_sems.at[1, chunk],
                partner,
            )

    def scatter_pair(chunk):
        if chunk in line_first:
            first_line(chunk)
            return
        def one(other):
            push(
                part_w.at[chunk, part(other * PAIR + 1 - column), :],
                pair_buf.at[chunk, part(other), :],
                scatter_sems.at[0, chunk],
                scatter_sems.at[1, chunk],
                partner,
            )

        loop(line, one)

    def scatter_line(chunk):
        if chunk in line_first:
            then_pair(chunk)
            return
        drain(pair_buf.at[chunk], scatter_sems.at[1, chunk])
        own = part_w[chunk, part(me), :].astype(f32)
        total[chunk] = own + pair_buf[chunk, part(row), :].astype(f32)

        def one(step, carry):
            other = line_peer(step)
            mine = part_w[chunk, part(other * PAIR + column), :].astype(f32)
            theirs = pair_buf[chunk, part(other), :].astype(f32)
            pair_buf[chunk, part(other), :] = (mine + theirs).astype(bf16)
            push(
                pair_buf.at[chunk, part(other), :],
                line_buf.at[chunk, part(step - 1), :],
                scatter_sems.at[2, chunk],
                scatter_sems.at[3, chunk],
                member(other),
            )
            return carry

        lax.fori_loop(1, line, one, 0)

    order = []
    lined = [0]

    def send_pair(chunk):
        order.append(chunk)
        scatter_pair(chunk)

    def line_ticked(count):
        while lined[0] < min(count, len(order)):
            scatter_line(order[lined[0]])
            lined[0] += 1

    def scatter_end(chunk):
        if chunk in line_first:
            last = line_buf.at[chunk, pl.ds(PAIR * rows, rows), :]
            drain(last, scatter_sems.at[1, chunk])
            total[chunk] += last[...].astype(f32)
            return
        drain(line_buf.at[chunk], scatter_sems.at[3, chunk])

        def one(step, carry):
            total[chunk] += line_buf[chunk, part(step - 1), :].astype(f32)
            return carry

        lax.fori_loop(1, line, one, 0)

    spread_sems, fold_sems = r.spread_sems, r.fold_sems

    def mine(spot_at):
        return pl.ds(pl.multiple_of(spot_at * own_lat, own_lat), own_lat)

    def mine_in(spot_at):
        return pl.ds(pl.multiple_of(spot_at * own_in, own_in), own_in)

    def some(half):
        return pl.ds(half * pairs, pairs)

    def slot(use, half):
        return use * tiles + half

    def spread_first(full, use, half):
        own = full.at[some(half), mine(spot), :]
        at = slot(use, half)
        push(own, own, spread_sems.at[at, 0], spread_sems.at[at, 1], to_row)
        push(own, own, spread_sems.at[at, 2], spread_sems.at[at, 3], to_core)

    def spread_next(full, use, half):
        got = full.at[some(half), mine(spot_row), :]
        at = slot(use, half)
        drain(got, spread_sems.at[at, 1])
        push(got, got, spread_sems.at[at, 4], spread_sems.at[at, 5], to_core)

    def spread_last(full, use, half):
        like = full.at[some(half), mine(spot), :]
        drain(like, spread_sems.at[slot(use, half), 3])
        drain(like, spread_sems.at[slot(use, half), 5])

    def spread_sent(full, use, half):
        for which in (0, 2, 4):
            drain(full.at[some(half), mine(spot), :], spread_sems.at[slot(use, half), which])

    fold_core, fold_row = r.fold_core, r.fold_row

    def fold_first(whole, use, half):
        for place, spot_at in enumerate((spot_core, spot_both)):
            push(
                whole.at[some(half), mine(spot_at), :],
                fold_core.at[FOLD_SLOT[use], place, some(half)],
                fold_sems.at[slot(use, half), 0],
                fold_sems.at[slot(use, half), 1],
                to_core,
            )

    def fold_next(whole, use, half):
        drain(fold_core.at[FOLD_SLOT[use], :, some(half)], fold_sems.at[slot(use, half), 1])
        for group in range(half * pairs, half * pairs + pairs):
            near = whole[group, mine(spot_row), :].astype(f32)
            far = fold_core[FOLD_SLOT[use], 1, group].astype(f32)
            whole[group, mine(spot_row), :] = (near + far).astype(bf16)
        push(
            whole.at[some(half), mine(spot_row), :],
            fold_row.at[FOLD_SLOT[use], some(half)],
            fold_sems.at[slot(use, half), 2],
            fold_sems.at[slot(use, half), 3],
            to_row,
        )

    def fold_last(use, half):
        drain(fold_row.at[FOLD_SLOT[use], some(half)], fold_sems.at[slot(use, half), 3])

    def folded(whole, use, group):
        near = whole[group, mine(spot), :].astype(f32) + fold_core[FOLD_SLOT[use], 0, group].astype(f32)
        return near + fold_row[FOLD_SLOT[use], group].astype(f32)

    def fold_sent(use, half):
        drain(fold_core.at[FOLD_SLOT[use], :, some(half)], fold_sems.at[slot(use, half), 0])
        drain(fold_row.at[FOLD_SLOT[use], some(half)], fold_sems.at[slot(use, half), 2])

    in_sems, in_fold_sems = r.in_sems, r.in_fold_sems
    normed_in = r.normed_in

    def in_first(group):
        own = normed_in.at[group, mine_in(spot), :]
        push(own, own, in_sems.at[group, 0], in_sems.at[group, 1], to_row)
        push(own, own, in_sems.at[group, 2], in_sems.at[group, 3], to_core)

    def in_next(group):
        got = normed_in.at[group, mine_in(spot_row), :]
        drain(got, in_sems.at[group, 1])
        push(got, got, in_sems.at[group, 4], in_sems.at[group, 5], to_core)

    def in_last(group):
        like = normed_in.at[group, mine_in(spot), :]
        drain(like, in_sems.at[group, 3])
        drain(like, in_sems.at[group, 5])

    def in_sent(group):
        for which in (0, 2, 4):
            drain(normed_in.at[group, mine_in(spot), :], in_sems.at[group, which])

    in_core, in_row = r.in_core, r.in_row
    ins = normed_in.shape[1]
    blocks, stacked = depth // width, depth // ins

    def dn_in(group, piece, at):
        first = piece % stacked * ins
        if not isinstance(piece, int):
            first = pl.multiple_of(first, ins)
        index = UP + (group * blocks + piece) // stacked
        return full_w.at[index, pl.ds(first + at.start, at.size), :]

    def in_fold_first(group):
        for place, spot_at in enumerate((spot_core, spot_both)):
            for piece in range(blocks):
                push(
                    dn_in(group, piece, mine_in(spot_at)),
                    in_core.at[group, place, piece],
                    in_fold_sems.at[group, 0],
                    in_fold_sems.at[group, 1],
                    to_core,
                )

    def in_fold_next(group):
        drain(in_core.at[group], in_fold_sems.at[group, 1])
        for piece in range(blocks):
            own = dn_in(group, piece, mine_in(spot_row))
            own[...] = (own[...].astype(f32) + in_core[group, 1, piece].astype(f32)).astype(bf16)
            push(
                own,
                in_row.at[group, piece],
                in_fold_sems.at[group, 2],
                in_fold_sems.at[group, 3],
                to_row,
            )

    lat, inp, cot = r.lat, r.inp, r.cot
    all_gains = (r.gain_input, r.gain_cross, r.gain_self, r.gain_mlp)

    def gain(index):
        return all_gains[index][...]

    def lanes(index, size=width):
        return pl.ds(pl.multiple_of(index * size, size), size)

    def project(target, source, chunk, half):
        value = dot(flat(source[some(half)]), full_w[chunk])
        target[some(half)] = value.astype(bf16).reshape(pairs, -1, width)

    def project_back(target, terms, half):
        def one(piece):
            value = None
            for source, first, chunk in terms:
                term = dot_t(
                    flat(source[some(half), :, first : first + width]),
                    full_w[chunk, lanes(piece), :],
                )
                value = term if value is None else value + term
            target[some(half), :, lanes(piece)] = value.astype(bf16).reshape(pairs, -1, width)

        loop(blocks, one)

    def weight_grad(chunk, left, right, first=0, send=True):
        def one(index):
            value = None
            for group in range(0, groups, pairs):
                for_rows = pl.ds(group, pairs)
                term = t_dot(
                    flat(left[for_rows, :, lanes(index)]),
                    flat(right[for_rows, :, first : first + width]),
                )
                value = term if value is None else value + term
            part_w[chunk, lanes(index), :] = value.astype(bf16)

        loop(blocks, one)
        if send:
            send_pair(chunk)

    def each(half, body):
        loop(pairs, lambda index: body(half * pairs + index))

    def attend(group, queries, keys, key_at, values, value_at, prob, target, masked):
        for head in range(heads):
            at = head * HEAD_DIM
            query = queries[group, :, at : at + HEAD_DIM]
            key = keys[group, :, key_at + at : key_at + at + HEAD_DIM]
            value = values[group, :, value_at + at : value_at + at + HEAD_DIM]
            scores = dot_t(query, key) * scaling
            if masked:
                scores = jnp.where(r.allow[group] > 0.5, scores, -1e30)
            grown = jnp.exp(scores - jnp.max(scores, axis=-1, keepdims=True))
            share = grown / jnp.sum(grown, axis=-1, keepdims=True)
            prob[group, head] = share
            target[group, :, at : at + HEAD_DIM] = dot(share.astype(bf16), value).astype(bf16)

    def attend_back(group, queries, keys, key_at, values, value_at, prob, grad, outs):
        (gq, gk, gk_at, gv, gv_at) = outs
        for head in range(heads):
            at = head * HEAD_DIM
            query = queries[group, :, at : at + HEAD_DIM]
            key = keys[group, :, key_at + at : key_at + at + HEAD_DIM]
            value = values[group, :, value_at + at : value_at + at + HEAD_DIM]
            back = grad[group, :, at : at + HEAD_DIM]
            share = prob[group, head]
            slope = dot_t(back, value)
            slope = share * (slope - jnp.sum(share * slope, axis=-1, keepdims=True))
            slope = slope.astype(bf16)
            gq[group, :, at : at + HEAD_DIM] = (dot(slope, key) * scaling).astype(bf16)
            gk[group, :, gk_at + at : gk_at + at + HEAD_DIM] = (
                t_dot(slope, query) * scaling
            ).astype(bf16)
            gv[group, :, gv_at + at : gv_at + at + HEAD_DIM] = t_dot(
                share.astype(bf16), back
            ).astype(bf16)

    gain_mine = r.gain_mine
    gain_mine[...] = jnp.zeros_like(gain_mine)

    def norm_back(rows_in, index, grad):
        shaped, scale = norm_parts(rows_in)
        gain_mine[index : index + 1, :] += jnp.sum(grad * shaped, axis=0, keepdims=True)
        grad = grad * gain(index)
        center = jnp.mean(grad, axis=-1, keepdims=True)
        along = jnp.mean(grad * shaped, axis=-1, keepdims=True)
        return (grad - center - shaped * along) * scale

    GAIN_INPUT, GAIN_CROSS, GAIN_SELF, GAIN_MLP = 0, 1, 2, 3

    def put(source, target, which):
        pltpu.make_async_copy(source, target, r.out_sems.at[which]).start()

    straight = [chunk for chunk in range(chunks) if chunk not in turned]
    for chunk in turned:
        weight, piece = holder(chunk)
        value = weight[piece * width : (piece + 1) * width, :].astype(f32)
        full_w[chunk, pl.ds(pl.multiple_of(me * rows, rows), rows), :] = value.T.astype(bf16)
    for chunk in straight:
        pltpu.make_async_copy(shard(chunk), block(chunk, me), r.own_sem).start()
    for chunk in range(chunks):
        if chunk < ahead or chunk in twice:
            gather_pair(chunk)
    for chunk in range(min(4, chunks)):
        gather_start(chunk)
    halves = range(tiles)

    def lat_rows(group):
        shaped, _ = norm_parts(lat[group].astype(f32))
        r.normed_lat[group, mine(spot), :] = (shaped * gain(GAIN_CROSS)).astype(bf16)

    for half in halves:
        each(half, lat_rows)
        spread_first(r.normed_lat, 0, half)

    def in_rows(group):
        shaped, _ = norm_parts(inp[group].astype(f32))
        normed_in[group, mine_in(spot), :] = (shaped * gain(GAIN_INPUT)).astype(bf16)
        in_first(group)

    for group in range(groups):
        in_rows(group)
        if group < 3:
            ticked(group + 1)
    r.spread_out[:, mine(spot), :] = cot[...]
    for half in halves:
        spread_first(r.spread_out, 3, half)
    for half in halves:
        spread_next(r.normed_lat, 0, half)
    in_next(0)
    drain(full_w.at[pl.ds(0, len(straight)), pl.ds(0, rows), :], r.own_sem)
    positions = lax.broadcasted_iota(jnp.int32, (1, ins), 1)
    for group in range(groups):
        allowed = (positions < r.counts[group]) & (
            (r.mask[group : group + 1, :] == 1) | (positions == 0)
        )
        r.allow[group] = allowed.astype(f32)
    ticked(4)
    have_weights(QC)
    for half in halves:
        spread_last(r.normed_lat, 0, half)
        project(r.q_one, r.normed_lat, QC, half)
    if groups > 1:
        in_next(1)
    have_weights(KC)
    have_weights(VC)
    keys = r.keys
    piece_rows = min(256, ins)

    def key_rows(group):
        in_last(group)
        for piece in range(ins // piece_rows):
            at = slice(piece * piece_rows, piece * piece_rows + piece_rows)
            keys[group, at, :width] = dot(normed_in[group, at, :], full_w[KC]).astype(bf16)
            keys[group, at, width:] = dot(normed_in[group, at, :], full_w[VC]).astype(bf16)
        attend(group, r.q_one, keys, 0, keys, width, r.prob_one, r.o_one, True)

    for group in range(groups):
        key_rows(group)
        ticked(6 + group)
        if 2 + group < groups:
            in_next(2 + group)
        half = group // pairs
        if group % pairs == pairs - 1:
            if half == 0:
                have_weights(OC)
            project_back(r.partial, [(r.o_one, 0, OC)], half)
            fold_first(r.partial, 0, half)
        elif half > 0:
            fold_next(r.partial, 0, half - 1)
    for half in halves:
        spread_next(r.spread_out, 3, half)
    for half in range(tiles - 1 if pairs > 1 else 0, tiles):
        fold_next(r.partial, 0, half)

    def one_rows(group):
        rows_now = lat[group].astype(f32) + folded(r.partial, 0, group)
        r.hidden_one[group] = rows_now
        shaped, _ = norm_parts(rows_now)
        r.normed_two[group, mine(spot), :] = (shaped * gain(GAIN_SELF)).astype(bf16)

    for half in halves:
        fold_last(0, half)
        each(half, one_rows)
        spread_first(r.normed_two, 1, half)
        ticked(10 + half)
    for half in halves:
        spread_next(r.normed_two, 1, half)
    have_weights(QS)
    have_weights(KS)
    have_weights(VS)

    def self_rows(group):
        attend(group, r.q_two, r.k_two, 0, r.v_two, 0, r.prob_two, r.o_two, False)

    for half in halves:
        spread_last(r.normed_two, 1, half)
        for target, chunk in ((r.q_two, QS), (r.k_two, KS), (r.v_two, VS)):
            project(target, r.normed_two, chunk, half)
        each(half, self_rows)
        if half == 0:
            have_weights(OS)
        ticked(12 + half)
        fold_sent(0, half)
        project_back(r.partial, [(r.o_two, 0, OS)], half)
        fold_first(r.partial, 1, half)
        if half > 0:
            fold_next(r.partial, 1, half - 1)
    fold_next(r.partial, 1, tiles - 1)
    ticked(14)

    def two_rows(group):
        rows_now = r.hidden_one[group] + folded(r.partial, 1, group)
        r.hidden_two[group] = rows_now
        shaped, _ = norm_parts(rows_now)
        r.normed_three[group, mine(spot), :] = (shaped * gain(GAIN_MLP)).astype(bf16)

    for half in halves:
        fold_last(1, half)
        each(half, two_rows)
        spread_first(r.normed_three, 2, half)
        ticked(15 + half)
    for half in halves:
        spread_next(r.normed_three, 2, half)

    def up_rows(half, at):
        pre = dot(flat(r.normed_three[some(half)]), full_w[UP + at])
        r.pre[some(half), :, at * width : (at + 1) * width] = pre.reshape(pairs, -1, width)
        r.act[some(half), :, at * width : (at + 1) * width] = (
            (pre * gelu_parts(pre)).astype(bf16).reshape(pairs, -1, width)
        )

    for half in halves:
        spread_last(r.normed_three, 2, half)
        spread_last(r.spread_out, 3, half)
    for at in range(downs):
        have_weights(UP + at)
        for half in halves:
            up_rows(half, at)
        ticked(UP + downs + 4 + at)
        weight_grad(down + at, r.spread_out, r.act, at * width, send=False)

    def down_rows(half, at):
        back = dot(flat(r.spread_out[some(half)]), full_w[down + at])
        pre = flat(r.pre[some(half), :, at * width : (at + 1) * width])
        r.grad_pre[some(half), :, at * width : (at + 1) * width] = (
            (back * gelu_slope(pre)).astype(bf16).reshape(pairs, -1, width)
        )

    for at in range(downs):
        if at == downs - 1:
            ticked(chunks + hops)
            for other in range(downs):
                send_pair(down + other)
            order.insert(1, order.pop(0))
        have_weights(down + at)
        for half in halves:
            down_rows(half, at)
        if at < downs - 1:
            weight_grad(UP + at, r.normed_three, r.grad_pre, at * width, send=False)
    for half in halves:
        fold_sent(1, half)
        project_back(
            r.partial, [(r.grad_pre, at * width, UP + at) for at in range(downs)], half
        )
        fold_first(r.partial, 2, half)
    line_ticked(1)
    for at in range(downs - 1):
        send_pair(UP + at)
    weight_grad(UP + downs - 1, r.normed_three, r.grad_pre, (downs - 1) * width)
    for half in halves:
        fold_next(r.partial, 2, half)
    for half in halves:
        project_back(
            r.partial_out, [(r.act, at * width, down + at) for at in range(downs)], half
        )
        fold_first(r.partial_out, 3, half)
    line_ticked(2)

    def back_two(group):
        grad = folded(r.partial, 2, group)
        value = cot[group].astype(f32) + norm_back(r.hidden_two[group], GAIN_MLP, grad)
        r.grad_two[group] = value
        r.spread_two[group, mine(spot), :] = value.astype(bf16)

    for half in halves:
        fold_last(2, half)
        each(half, back_two)
        spread_first(r.spread_two, 4, half)
    line_ticked(3)
    for half in halves:
        spread_next(r.spread_two, 4, half)
    for half in halves:
        fold_next(r.partial_out, 3, half)
    line_ticked(4)

    def self_back(group):
        attend_back(
            group,
            r.q_two,
            r.k_two,
            0,
            r.v_two,
            0,
            r.prob_two,
            r.grad_att,
            (r.gq_two, r.gk_two, 0, r.gv_two, 0),
        )

    for half in halves:
        spread_last(r.spread_two, 4, half)
        project(r.grad_att, r.spread_two, OS, half)
        each(half, self_back)
        fold_sent(2, half)
        project_back(
            r.partial, [(r.gq_two, 0, QS), (r.gk_two, 0, KS), (r.gv_two, 0, VS)], half
        )
        fold_first(r.partial, 4, half)
        if half > 0:
            fold_next(r.partial, 4, half - 1)
        line_ticked(5 + half)
    weight_grad(OS, r.spread_two, r.o_two)
    fold_next(r.partial, 4, tiles - 1)
    weight_grad(QS, r.normed_two, r.gq_two)
    line_ticked(7)
    weight_grad(KS, r.normed_two, r.gk_two)

    def back_one(group):
        grad = folded(r.partial, 4, group)
        value = r.grad_two[group] + norm_back(r.hidden_one[group], GAIN_SELF, grad)
        r.grad_one[group] = value
        r.spread_one[group, mine(spot), :] = value.astype(bf16)

    for half in halves:
        fold_last(4, half)
        each(half, back_one)
        spread_first(r.spread_one, 5, half)
    line_ticked(8)
    weight_grad(VS, r.normed_two, r.gv_two)
    for half in halves:
        spread_next(r.spread_one, 5, half)
    line_ticked(9)

    def out_rows(group):
        r.block_out[group] = (
            r.hidden_two[group] + folded(r.partial_out, 3, group)
        ).astype(bf16)

    for chunk in range(chunks):
        gather_sent(chunk)

    def cross_back(group):
        attend_back(
            group,
            r.q_one,
            keys,
            0,
            keys,
            width,
            r.prob_one,
            r.grad_att,
            (r.gq_one, r.grad_keys, 0, r.grad_keys, width),
        )

    def in_back(group):
        for at in range(0, ins, piece_rows):

            def one(piece):
                value = dot_t(
                    r.grad_keys[group, at : at + piece_rows, :width], full_w[KC, lanes(piece), :]
                ) + dot_t(
                    r.grad_keys[group, at : at + piece_rows, width:], full_w[VC, lanes(piece), :]
                )
                dn_in(group, piece, pl.ds(at, piece_rows))[...] = value.astype(bf16)

            loop(blocks, one)
        in_fold_first(group)

    for half in halves:
        spread_last(r.spread_one, 5, half)
        if half == tiles - 1:
            weight_grad(OC, r.spread_one, r.o_one)
        project(r.grad_att, r.spread_one, OC, half)
        each(half, cross_back)
        each(half, in_back)
        line_ticked(10 + half)
    for half in halves[:1]:
        each(half, in_fold_next)
    line_ticked(12)
    weight_grad(KC, normed_in, r.grad_keys, 0)
    for half in halves[1:]:
        each(half, in_fold_next)
    weight_grad(VC, normed_in, r.grad_keys, width)
    line_ticked(13)
    for half in halves:
        fold_sent(4, half)
        project_back(r.partial, [(r.gq_one, 0, QC)], half)
        fold_first(r.partial, 5, half)
    weight_grad(QC, r.normed_lat, r.gq_one)
    for half in halves:
        fold_next(r.partial, 5, half)
    line_ticked(14)
    for half in halves:
        fold_last(3, half)
        each(half, out_rows)
        put(r.block_out.at[some(half)], r.out_block.at[some(half)], 0)
    for group in range(groups):
        in_sent(group)

    def in_final(group):
        drain(in_row.at[group], in_fold_sems.at[group, 3])
        parts = []
        for piece in range(blocks):
            near = dn_in(group, piece, mine_in(spot))[...].astype(f32)
            near = near + in_core[group, 0, piece].astype(f32)
            parts.append(near + in_row[group, piece].astype(f32))
        grad = jnp.concatenate(parts, axis=-1)
        r.grad_in[group] = norm_back(inp[group].astype(f32), GAIN_INPUT, grad)

    line_ticked(15)
    each(0, in_final)
    put(r.grad_in.at[some(0)], r.out_in.at[some(0)], 2)
    line_ticked(16)
    for half in halves[1:]:
        each(half, in_final)
        put(r.grad_in.at[some(half)], r.out_in.at[some(half)], 2)

    def lat_back(group):
        grad = folded(r.partial, 5, group)
        r.grad_lat[group] = r.grad_one[group] + norm_back(
            lat[group].astype(f32), GAIN_CROSS, grad
        )

    for half in halves:
        fold_last(5, half)
        each(half, lat_back)
        put(r.grad_lat.at[some(half)], r.out_lat.at[some(half)], 1)
    gain_sems, gain_head = r.gain_sems, r.gain_head
    gain_sum, gain_recv, gain_line = r.gain_sum, r.gain_recv, r.gain_line
    spots = r.normed_in.shape[1] // own_in
    gain_head[spot] = gain_mine[...]
    for place in (to_row, to_both, to_core):
        own = gain_head.at[spot]
        push(own, own, gain_sems.at[0, 0], gain_sems.at[1, 0], place)
    drain(gain_head.at[pl.ds(0, spots - 1)], gain_sems.at[1, 0])
    whole = gain_head[0]
    for other in range(1, spots):
        whole = whole + gain_head[other]
    gain_sum[...] = whole
    push(gain_sum, gain_recv, gain_sems.at[0, 1], gain_sems.at[1, 1], partner)
    drain(gain_recv, gain_sems.at[1, 1])
    gain_line[row] = gain_sum[...] + gain_recv[...]

    def gain_send(step, carry):
        push(
            gain_line.at[row],
            gain_line.at[row],
            gain_sems.at[0, 3],
            gain_sems.at[1, 3],
            member(line_peer(step)),
        )
        return carry

    lax.fori_loop(1, line, gain_send, 0)
    for chunk in order:
        scatter_end(chunk)
        put(total.at[chunk], r.out_w.at[chunk], 3)
    drain(gain_line.at[pl.ds(0, line - 1)], gain_sems.at[1, 3])
    whole = gain_line[0]
    for other in range(1, line):
        whole = whole + gain_line[other]
    r.grad_gain[...] = whole

    for chunk in order:
        if chunk in line_first:
            drain(line_buf.at[chunk, pl.ds(0, rows), :], scatter_sems.at[0, chunk])
            drain(line_like(chunk), scatter_sems.at[2, chunk])
        else:
            drain(pair_buf.at[chunk], scatter_sems.at[0, chunk])
            drain(line_buf.at[chunk], scatter_sems.at[2, chunk])
    spreads = (
        r.normed_lat,
        r.normed_two,
        r.normed_three,
        r.spread_out,
        r.spread_two,
        r.spread_one,
    )
    for use, full in enumerate(spreads):
        for half in halves:
            spread_sent(full, use, half)
    for half in halves:
        fold_sent(3, half)
        fold_sent(5, half)

    def in_folds_sent(group):
        drain(in_core.at[group], in_fold_sems.at[group, 0])
        drain(in_row.at[group], in_fold_sems.at[group, 2])

    loop(groups, in_folds_sent)
    for which, value in enumerate((r.block_out, r.grad_lat, r.grad_in, total)):
        drain(value, r.out_sems.at[which])
    drain(gain_head.at[pl.ds(0, spots - 1)], gain_sems.at[0, 0])
    drain(gain_recv, gain_sems.at[0, 1])
    drain(gain_line.at[pl.ds(0, line - 1)], gain_sems.at[0, 3])


def run_block(members, turned, *args):
    lat, inp, cot, mask = args[:4]
    weights = args[9:]
    groups, own_lat, depth = lat.shape
    own_in = inp.shape[1]
    width = CHUNK
    rows = depth // members
    ins = mask.shape[1]
    spots = ins // own_in
    latents = own_lat * spots
    sizes = [weight.size // (rows * width) for weight in weights]
    chunks = sum(sizes)
    hidden = sizes[-1] * width
    line = members // PAIR
    heads = width // HEAD_DIM
    tiles = groups // 2 if groups % 2 == 0 else groups
    vmem = pltpu.VMEM
    vspec = pl.BlockSpec(memory_space=pltpu.VMEM)
    anywhere = pl.BlockSpec(memory_space=pl.ANY)
    narrow = vmem((groups, latents, width), bf16)
    full = vmem((groups, latents, depth), bf16)
    own = vmem((groups, own_lat, depth), f32)
    gain_shape = (8, depth)
    dma = pltpu.SemaphoreType.DMA
    wspecs = [
        vspec if turned and index in TURNED else anywhere for index in range(len(weights))
    ]
    return pl.pallas_call(
        functools.partial(block_kernel, members, turned),
        out_shape=(
            jax.ShapeDtypeStruct((groups, own_lat, depth), bf16),
            jax.ShapeDtypeStruct((groups, own_lat, depth), f32),
            jax.ShapeDtypeStruct((groups, own_in, depth), f32),
            jax.ShapeDtypeStruct(gain_shape, f32),
            jax.ShapeDtypeStruct((chunks, rows, width), f32),
        ),
        in_specs=[vspec] * 4
        + [pl.BlockSpec(memory_space=pltpu.SMEM)]
        + [vspec] * 4
        + wspecs,
        out_specs=(anywhere,) * 3 + (vspec, anywhere),
        scratch_shapes=[
            vmem((groups, 1, ins), f32),
            vmem((groups, own_lat, depth), bf16),
            vmem((groups, own_lat, depth), f32),
            vmem((groups, own_in, depth), f32),
            vmem((chunks, rows, width), f32),
            dma((4,)),
            vmem((chunks, depth, width), bf16),
            vmem((chunks, depth, width), bf16),
            vmem((chunks, line * rows, width), bf16),
            vmem((chunks, (line - 1) * rows, width), bf16),
            vmem((groups, ins, depth), bf16),
            full,
            full,
            full,
            vmem((groups, ins, 2 * width), bf16),
            vmem((groups, ins, 2 * width), bf16),
        ]
        + [narrow] * 11
        + [
            vmem((groups, heads, latents, ins), f32),
            vmem((groups, heads, latents, latents), f32),
            vmem((groups, latents, hidden), f32),
            vmem((groups, latents, hidden), bf16),
            vmem((groups, latents, hidden), bf16),
            full,
            full,
            full,
            own,
            own,
            own,
            own,
            full,
            full,
            vmem((2, 2, groups, own_lat, depth), bf16),
            vmem((2, groups, own_lat, depth), bf16),
            vmem((groups, 2, depth // width, own_in, width), bf16),
            vmem((groups, depth // width, own_in, width), bf16),
            vmem(gain_shape, f32),
            vmem((spots,) + gain_shape, f32),
            vmem(gain_shape, f32),
            vmem(gain_shape, f32),
            vmem((line,) + gain_shape, f32),
            dma,
            dma((4, chunks)),
            dma((4, chunks)),
            dma((6 * tiles, 6)),
            dma((6 * tiles, 4)),
            dma((groups, 6)),
            dma((groups, 4)),
            dma((chunks, 2, min(line, 4) - 1)),
            dma((2, 4)),
        ],
        compiler_params=pltpu.CompilerParams(
            collective_id=0, has_side_effects=True, vmem_limit_bytes=VMEM_TOP
        ),
    )(*args)


TURNED = (3, 7, 9)


def finish_kernel(sizes, turned, *refs):
    count = len(sizes)
    ins, outs = refs[:5], refs[5 : 12 + count]
    held, parts, gain_rows, flipped, in_sems, out_sems = refs[12 + count :]
    chunks, rows, width = parts.shape
    here = held
    started = []

    def begin(source, target):
        copy = pltpu.make_async_copy(source, target, out_sems.at[len(started)])
        copy.start()
        started.append(copy)

    passing = (ins[0], ins[1], ins[2], ins[3])
    loads = [
        pltpu.make_async_copy(source, target, in_sems.at[index])
        for index, (source, target) in enumerate(zip(passing, here))
    ]
    pieces = [
        pltpu.make_async_copy(ins[4].at[chunk], parts.at[chunk], in_sems.at[4 + chunk])
        for chunk in range(chunks)
    ]
    loads[2].start()
    for piece in pieces:
        piece.start()
    for index in (1, 0, 3):
        loads[index].start()
    loads[2].wait()
    begin(here[2], outs[2])
    chunk, turn = 0, 0
    for index, size in enumerate(sizes):
        for piece in range(size):
            pieces[chunk].wait()
            out = outs[7 + index]
            at = slice(piece * width, (piece + 1) * width)
            if chunk in turned:
                flipped[turn] = parts[chunk].T
                begin(flipped.at[turn], out.at[at, :])
                turn += 1
            else:
                begin(parts.at[chunk], out.at[:, at])
            chunk += 1
    for index in (1, 0):
        loads[index].wait()
        begin(here[index], outs[index])
    loads[3].wait()
    for index in range(4):
        gain_rows[index] = here[3][index : index + 1, :]
        begin(gain_rows.at[index], outs[3 + index])
    for copy in started:
        copy.wait()


def finish(turned, sizes, block_out, grad_lat, grad_in, grad_gain, grad_w):
    chunks, rows, width = grad_w.shape
    depth = block_out.shape[-1]
    passing = (block_out, grad_lat, grad_in)
    shapes = [jax.ShapeDtypeStruct(value.shape, value.dtype) for value in passing]
    shapes += [jax.ShapeDtypeStruct((1, depth), f32)] * 4
    first = 0
    for size in sizes:
        shape = (width * size, rows) if first in turned else (rows, width * size)
        shapes.append(jax.ShapeDtypeStruct(shape, f32))
        first += size
    anywhere = pl.BlockSpec(memory_space=pl.ANY)
    vmem, dma = pltpu.VMEM, pltpu.SemaphoreType.DMA
    return pl.pallas_call(
        functools.partial(finish_kernel, sizes, turned),
        out_shape=tuple(shapes),
        in_specs=[anywhere] * 5,
        out_specs=(anywhere,) * len(shapes),
        scratch_shapes=[
            [vmem(value.shape, value.dtype) for value in passing + (grad_gain,)],
            vmem(grad_w.shape, f32),
            vmem((4, 1, depth), f32),
            vmem((max(len(turned), 1), width, rows), f32),
            dma((4 + chunks,)),
            dma((7 + chunks,)),
        ],
        compiler_params=pltpu.CompilerParams(vmem_limit_bytes=VMEM_TOP),
    )(block_out, grad_lat, grad_in, grad_gain, grad_w)


def per_device(members, *args):
    (latents, inputs, input_masks, valid_counts) = args[:4]
    gain_set, weights, out_cotangent = args[4:8], args[8:18], args[18]
    depth = latents.shape[2]
    rows = depth // members
    inside = rows % 128 == 0
    sizes = [weight.size // (rows * CHUNK) for weight in weights]
    turned, first = [], 0
    for index, size in enumerate(sizes):
        if inside and index in TURNED:
            turned += range(first, first + size)
        first += size
    turned = tuple(turned)
    if not inside:
        weights = [w.T if index in TURNED else w for index, w in enumerate(weights)]
    gains = [gain.reshape(1, depth) for gain in gain_set]
    done = run_block(
        members,
        turned,
        latents,
        inputs,
        out_cotangent,
        input_masks,
        valid_counts,
        *gains,
        *weights,
    )
    done = finish(turned, sizes, *done)
    grads = done[7:]
    if not inside:
        grads = [g.T if index in TURNED else g for index, g in enumerate(grads)]
    return (*done[:3], *[gain.reshape(depth) for gain in done[3:7]], *grads)


def solution(mesh):
    rows_first = P("dp", "head")
    cols_first = P("head", "dp")
    tokens = P("dp", "head", None)
    weight_specs = tuple(cols_first if index in TURNED else rows_first for index in range(10))
    in_specs = (tokens, tokens, P("dp", None), P("dp"), P(), P(), P(), P(), *weight_specs, tokens)
    out_specs = (tokens, tokens, tokens, P(), P(), P(), P(), *weight_specs)
    return jax.shard_map(
        functools.partial(per_device, mesh.shape["dp"]),
        mesh=mesh,
        in_specs=in_specs,
        out_specs=out_specs,
        check_vma=False,
    )
```
